32 devices in a mesh: grp: 2 (over x), seq: 16 (over z, y, core).
Axes of the slice: x: 2, y: 2, z: 4, core: 2. Of those that a mesh axis runs over, the one named last changes fastest.
Arguments:
- queries: bfloat16 [8192, 8192], P(('grp', 'seq')), parts along dimension 0, may hold values from -6 to 6
- keys_in: bfloat16 [8192, 8192], P(('grp', 'seq')), parts along dimension 0, may hold values from -0.375 to 0.375
- values_in: bfloat16 [8192, 8192], P(('grp', 'seq')), parts along dimension 0, may hold values from -6 to 6
- log_decay: bfloat16 [8192, 64], P(('grp', 'seq')), parts along dimension 0, may hold values from -2 to 0, as said below
- gate_logits: bfloat16 [8192, 8192], P(('grp', 'seq')), parts along dimension 0, may hold values from -6 to 6
- norm_gain: float32 [8192], replicated, may hold values from 0.1 to 1.9
- doc_lengths: int32 [16], P('grp'), parts along dimension 0, may hold values from 1 to 2048, 4096 in all
Outputs:
- attended: bfloat16 [8192, 8192], P(('grp', 'seq')), parts along dimension 0
- final_state: float32 [128, 128, 128], P(('grp', 'seq')), parts along dimension 0
The draws below stay inside these ranges and needn't reach their ends.
There are 2 independent parts, one for each index of `grp`. The reference program is written for one: setup_inputs(seed, part) draws one part's arguments, and reference() takes and returns one part's arrays. A program takes and returns all parts, laid end to end along the dimension named above; an argument that names none is the same for every part. Nothing has to cross between parts.
Inputs may be any that keep to these rules, and one draw needn't show every extreme that they name: log_decay is negative. `doc_lengths`: the 8 lengths are positive and sum to 4096.
All inputs are finite; a program needn't handle non-finite values.
Results may differ from the reference program's by a relative error of at most 0.0049.
Values may be sent and summed in bfloat16 or wider, within the bound.
A program may use at most 320 MiB of HBM per device.

```python
import math
import jax
import jax.numpy as jnp
import numpy as np
from jax import lax

HEADS = 64
HEAD_DIM = 128
SPAN = 256
DOCS = 8
TOK_DEV = 256
PACKED_TOKENS = 4096


def draw_log_decay(key, part):
    fast_share = 0.5
    fast = jax.random.uniform(jax.random.fold_in(key, 11), (HEADS,)) < fast_share
    fast_rate = jax.random.uniform(jax.random.fold_in(key, 12), (HEADS,), minval=1.0 / 40.0, maxval=1.0 / 25.0)
    slow_rate = jax.random.uniform(jax.random.fold_in(key, 13), (HEADS,), minval=0.1, maxval=0.3) * 2.302585 / PACKED_TOKENS
    decay_rate = jnp.where(fast, fast_rate, slow_rate)
    token_decay_factor = jax.random.uniform(jax.random.fold_in(key, 14), (PACKED_TOKENS, HEADS), minval=0.5, maxval=1.5)
    block_decay_factor = jax.random.uniform(jax.random.fold_in(key, 15), (PACKED_TOKENS // TOK_DEV, 1, HEADS), minval=0.5, maxval=1.5)
    block_decay_factor = jnp.broadcast_to(block_decay_factor, (PACKED_TOKENS // TOK_DEV, TOK_DEV, HEADS)).reshape(PACKED_TOKENS, HEADS)
    spike_positions = jax.random.randint(jax.random.fold_in(key, 16), (2,), 0, PACKED_TOKENS)
    retention = jax.random.uniform(jax.random.fold_in(key, 17), (2, HEADS), minval=0.5, maxval=0.8)
    spike_flags = (jnp.arange(PACKED_TOKENS)[:, None] == spike_positions[None, :]).astype(jnp.float32)
    spike_log_decay = jnp.dot(spike_flags, jnp.log(retention))
    return (-decay_rate[None, :] * token_decay_factor * block_decay_factor + spike_log_decay).astype(jnp.bfloat16)


def block_levels(rng, shape, shards, low, largest):
    def one(axis_at, blocks):
        heights = jax.random.uniform(jax.random.fold_in(jax.random.fold_in(rng, 6), axis_at), (blocks,), jnp.float32, low / len(shards), largest / len(shards))
        return jnp.repeat(jnp.exp(heights), shape[axis_at] // blocks).reshape((-1,) + (1,) * (len(shape) - axis_at - 1))

    loudness = one(*shards[0])
    for cut in shards[1:]:
        loudness = loudness * one(*cut)
    return loudness


def profile(amount, total, bound, slope):
    portions = [(1 << 20) // math.isqrt(grade ** slope) + 1 for grade in range(2, amount + 1)]
    spare, counts = total - bound - (amount - 1), [1] * (amount - 1)
    while spare > 0:
        free = [i for i in range(amount - 1) if counts[i] < bound]
        pool, left = sum([portions[i] for i in free]), spare
        for i in free:
            extra = min(bound - counts[i], max(1, left * portions[i] // pool), spare)
            counts[i] = counts[i] + extra
            spare = spare - extra
    return np.array([bound] + counts)


def ragged(own_key, amount, total, most, skew):
    if amount == 2:
        one = jax.random.randint(own_key, (), max(1, total - most), min(most, total - 1) + 1)
        return jnp.stack([one, total - one])
    sizes = jnp.asarray(profile(amount, total, most, skew), jnp.int32)
    couples = (amount - 1) // 2
    donor, taker = sizes[1:1 + 2 * couples:2], sizes[2:2 + 2 * couples:2]
    slack = jnp.minimum(donor - 1, most - taker)
    moved = jax.random.randint(jax.random.fold_in(own_key, 1), (couples,), 0, 1 << 20) % (slack + 1)
    sizes = sizes.at[1:1 + 2 * couples:2].set(donor - moved).at[2:2 + 2 * couples:2].set(taker + moved)
    return sizes[jax.random.permutation(jax.random.fold_in(own_key, 2), amount)]


def noise(rng, dims, width, limit, split=(), kind=jnp.bfloat16):
    result = jax.random.normal(rng, dims, jnp.float32) * width
    if len(split) > 0:
        result = block_levels(rng, dims, split, -0.22, 0.18) * result
    return jnp.clip(result, min=-limit, max=limit).astype(kind)


def setup_inputs(seed: int = 0, part: int = 0) -> dict:
    streams_of = jax.random.split(jax.random.key(seed), 8)
    part_splits = jax.random.split(jax.random.fold_in(streams_of[7], part), 8)
    queries = noise(part_splits[0], (PACKED_TOKENS, HEADS * HEAD_DIM), 1.0, 6.0, ((0, 16),))
    keys_in = noise(part_splits[1], (PACKED_TOKENS, HEADS * HEAD_DIM), 0.0625, 0.375, ((0, 16),))
    values_in = noise(part_splits[2], (PACKED_TOKENS, HEADS * HEAD_DIM), 1.0, 6.0, ((0, 16),))
    log_decay = draw_log_decay(jax.random.fold_in(jax.random.fold_in(streams_of[7], part), 71), part)
    gate_logits = noise(part_splits[4], (PACKED_TOKENS, HEADS * HEAD_DIM), 1.0, 6.0, ((0, 16),))
    norm_gain = jnp.clip(1.0 + 0.18 * jax.random.normal(streams_of[5], (HEADS * HEAD_DIM,), jnp.float32), 0.1, 1.9)
    doc_lengths = ragged(part_splits[6], DOCS, PACKED_TOKENS, PACKED_TOKENS // 2, 2).astype(jnp.int32)
    return {"queries": queries, "keys_in": keys_in, "values_in": values_in, "log_decay": log_decay, "gate_logits": gate_logits, "norm_gain": norm_gain, "doc_lengths": doc_lengths}


EPS = 1e-05

def doc_index(doc_lengths, positions):
    doc_ends = jnp.cumsum(doc_lengths).astype(jnp.int32)
    return lax.optimization_barrier(jnp.sum((positions[:, None] >= doc_ends[None, :]).astype(jnp.int32), axis=1)).astype(jnp.int32)

def reference(queries, keys_in, values_in, log_decay, gate_logits, norm_gain, doc_lengths):
    spans = PACKED_TOKENS // SPAN
    positions = jnp.arange(PACKED_TOKENS, dtype=jnp.int32)
    documents = doc_index(doc_lengths, positions).reshape(spans, SPAN)
    before = doc_index(doc_lengths, positions - 1).reshape(spans, SPAN)[:, 0]
    span_shape = (spans, SPAN, HEADS, HEAD_DIM)
    query_rows = queries.reshape(span_shape)
    key_rows = keys_in.reshape(span_shape)
    value_rows = values_in.reshape(span_shape)
    decay_rows = log_decay.astype(jnp.float32).reshape(spans, SPAN, HEADS)
    causal = jnp.arange(SPAN)[:, None] >= jnp.arange(SPAN)[None, :]

    def advance(state, batch_item):
        query_blk, key_blk, value_blk, decay_blk, doc_blk, prior_doc = batch_item
        cumulative = jnp.cumsum(decay_blk, axis=0)
        allowed = causal & (doc_blk[:, None] == doc_blk[None, :])
        cumul_heads = cumulative.T
        spread_log = jnp.where(allowed[None], cumul_heads[:, :, None] - cumul_heads[:, None, :], 0.0)
        decay_grid = jnp.where(allowed[None], jnp.exp(spread_log), 0.0)
        query_f = query_blk.astype(jnp.float32)
        key_f = key_blk.astype(jnp.float32)
        value_f = value_blk.astype(jnp.float32)
        scores = jnp.einsum('ihd,jhd->hij', query_f, key_f)
        weights = lax.optimization_barrier((scores * decay_grid).astype(jnp.bfloat16)).astype(jnp.float32)
        inside = jnp.einsum('hij,jhd->ihd', weights, value_f)
        carried = (doc_blk == prior_doc).astype(jnp.float32)
        across = jnp.einsum('ihd,hde->ihe', query_f, state, precision=lax.Precision.HIGHEST)
        across = across * (carried[:, None] * jnp.exp(cumulative))[:, :, None]
        closing_doc = (doc_blk == doc_blk[-1]).astype(jnp.float32)
        key_weight = closing_doc[:, None] * jnp.exp(cumulative[-1][None, :] - cumulative)
        weighted = lax.optimization_barrier((key_f * key_weight[:, :, None]).astype(jnp.bfloat16)).astype(jnp.float32)
        update = jnp.einsum('jhd,jhe->hde', weighted, value_f)
        factor = carried[-1] * jnp.exp(cumulative[-1])
        new_state = factor[:, None, None] * state + update
        return (new_state, inside + across)
    initial = jnp.zeros((HEADS, HEAD_DIM, HEAD_DIM), jnp.float32)
    final_state, outputs = lax.scan(advance, initial, (query_rows, key_rows, value_rows, decay_rows, documents, before))
    mixed = outputs.reshape(PACKED_TOKENS, HEADS * HEAD_DIM)
    inverse_rms = lax.rsqrt(lax.optimization_barrier(jnp.mean(mixed * mixed, axis=1, keepdims=True)) + EPS)
    gated = mixed * inverse_rms * norm_gain[None, :] * jax.nn.sigmoid(gate_logits.astype(jnp.float32))
    return (gated.astype(jnp.bfloat16), final_state)
```

```python
import functools
import math

import jax
import jax.numpy as jnp
from jax import lax
from jax.experimental import pallas as pl
from jax.experimental.pallas import tpu as pltpu
from jax.sharding import PartitionSpec as P

EPS = 1e-05
LOG2E = 1.4426950408889634
D = 128
GROUP = 4
CHUNKS = 8
CHAIN_LAG = 4
HOP_LAG = 2
E_LAG = 4
X_LAG = 2
FINISH_PARTS = 8
F32, BF16 = jnp.float32, jnp.bfloat16
MESH = pl.DeviceIdType.MESH


def dot(a, b, dims):
    return lax.dot_general(a, b, (dims, ((), ())), preferred_element_type=F32)


def kernel(
    n, heads, chunks,
    q_hbm, k_hbm, v_hbm, g_hbm, ld_hbm, gain_hbm, docs_hbm,
    out_s, ssq_s, fin_s,
    mix_s, gate_s, q_s, k_s, v_s, g_s, kt_s, ld_s, gain_s, docs_s, pen_s, cumt_s, kwt_s, cum_s, lead_s,
    fac_own, fac_core, fac_chip, fac_pair, u_own, u_core, u_mine, u_send, u_pair, s_in, s_out, e_send, e_half,
    x_send, ent,
    load_sem, small_sem, fac_ss, fac_rs, core_ss, core_rs, pair_ss, pair_rs, z_ss, z_rs, e_ss, e_rs,
    x_ss, x_rs, f_ss, f_rs, f_ls,
):
    tok = q_hbm.shape[0]
    hc = heads // chunks
    half = hc // 2
    w = half // 2
    planes = n // GROUP
    hn = heads // n
    g = math.gcd(w, hn)
    span = 2 * hn
    m = span // half
    me = lax.axis_index("seq")
    plane = me // GROUP
    r = me % GROUP
    y = r // 2
    c = r % 2
    core_peer = plane * GROUP + y * 2 + (1 - c)
    pair_peer = plane * GROUP + (1 - y) * 2 + c

    def send(src, dst, ss, rs, dev):
        return pltpu.make_async_remote_copy(
            src_ref=src, dst_ref=dst, send_sem=ss, recv_sem=rs,
            device_id={"seq": dev}, device_id_type=MESH,
        )

    def head0(j, yh):
        return (j // m) * (2 * span) + yh * span + (j % m) * half

    def hcols(j, yh):
        return pl.ds(pl.multiple_of(head0(j, yh) * D, half * D), half * D)

    def hcol(j, yh, hh):
        return pl.ds(pl.multiple_of((head0(j, yh) + hh) * D, D), D)

    def load(which, hbm, vm, j, yh):
        at = hcols(j, yh)
        return pltpu.make_async_copy(hbm.at[:, at], vm.at[:, at], load_sem.at[which, j, yh])

    def start_pair(a, a_hbm, a_vm, b, b_hbm, b_vm):
        def go(j, carry):
            for yh in range(2):
                load(a, a_hbm, a_vm, j, yh).start()
                load(b, b_hbm, b_vm, j, yh).start()
            return carry
        return go

    ld_copy = pltpu.make_async_copy(ld_hbm, ld_s.at[pl.ds(0, heads)], small_sem.at[0])
    docs_copy = pltpu.make_async_copy(docs_hbm, docs_s, small_sem.at[1])
    gain_copy = pltpu.make_async_copy(gain_hbm, gain_s, small_sem.at[2])
    ld_copy.start()
    docs_copy.start()
    lax.fori_loop(0, chunks, start_pair(0, k_hbm, k_s, 1, v_hbm, v_s), 0)

    barrier = pltpu.get_barrier_semaphore()
    for d in range(1, GROUP):
        pl.semaphore_signal(
            barrier, inc=1, device_id={"seq": plane * GROUP + (r + d) % GROUP}, device_id_type=MESH
        )

    @pl.when(plane > 0)
    def _():
        pl.semaphore_signal(barrier, inc=1, device_id={"seq": me - GROUP}, device_id_type=MESH)

    gain_copy.start()
    lax.fori_loop(0, chunks, start_pair(2, q_hbm, q_s, 3, g_hbm, g_s), 0)

    if heads < D:
        ld_s[pl.ds(heads, D - heads)] = jnp.zeros((D - heads, tok), BF16)
    base = me * tok
    row_i = lax.broadcasted_iota(jnp.int32, (tok, tok), 0)
    col_i = lax.broadcasted_iota(jnp.int32, (tok, tok), 1)
    causal = row_i >= col_i
    lanes = lax.broadcasted_iota(jnp.int32, (1, tok), 1)
    docs_copy.wait()
    n_docs = docs_s.shape[0]
    doc_row = jnp.zeros((1, tok), jnp.int32)
    before = jnp.int32(0)
    last = jnp.int32(0)
    end = jnp.int32(0)
    for d in range(n_docs):
        end = end + docs_s[d]
        doc_row = doc_row + jnp.where(lanes + base >= end, 1, 0)
        before = before + jnp.where(base - 1 >= end, 1, 0)
        last = last + jnp.where(base + tok - 1 >= end, 1, 0)
    closing = jnp.where(doc_row == last, 1.0, 0.0).astype(F32)
    ld_copy.wait()
    upper = jnp.where(row_i <= col_i, 1.0, 0.0).astype(BF16)
    cumt = dot(ld_s[pl.ds(0, heads)], upper, ((1,), (0,)))
    cumt_s[...] = LOG2E * cumt
    total = cumt[:, tok - 1:tok]
    kwt_s[...] = closing * jnp.exp(total - cumt)

    def updates(j):
        for yh in range(2):
            load(0, k_hbm, k_s, j, yh).wait()
            load(1, v_hbm, v_s, j, yh).wait()

    def update_math(j):
        for yh in range(2):
            for hh in range(half):
                h = head0(j, yh) + hh
                kt = k_s[:, hcol(j, yh, hh)].T
                kt_s[h] = kt
                wk = (kt.astype(F32) * kwt_s[pl.ds(h, 1), :]).astype(BF16)
                up = dot(wk, v_s[:, hcol(j, yh, hh)], ((1,), (0,)))
                u_own[j, hh // w, yh, hh % w] = up.astype(BF16)

    def core_copy(j):
        return send(u_own.at[j, 1 - c], u_core.at[j], core_ss.at[j], core_rs.at[j], core_peer)

    def pair_copy(j):
        return send(u_send.at[j], u_pair.at[j], pair_ss.at[j], pair_rs.at[j], pair_peer)

    def z_copy(j):
        return send(s_out.at[j], s_in.at[j], z_ss.at[j], z_rs.at[j], (me + GROUP) % n)

    def e_copy(j):
        return send(e_send.at[j], e_half.at[j, y], e_ss.at[j], e_rs.at[j], pair_peer)

    def x_copy(j):
        return send(x_send.at[j], ent.at[j, c], x_ss.at[j], x_rs.at[j], core_peer)

    def fac_core_copy():
        return send(fac_own, fac_core, fac_ss.at[0], fac_rs.at[0], core_peer)

    def fac_pair_copy():
        return send(fac_chip.at[c, 1 - y], fac_pair, fac_ss.at[1], fac_rs.at[1], pair_peer)

    def combine(j):
        core_copy(j).wait_recv()
        for k in range(w):
            for yo in range(2):
                at = pl.ds(j * w + k, 1)
                fa = jnp.where(c == 0, fac_core[c, yo, at, :], 1.0)
                fb = jnp.where(c == 0, 1.0, fac_own[c, yo, at, :])
                val = fa * u_own[j, c, yo, k].astype(F32) + fb * u_core[j, yo, k].astype(F32)

                @pl.when(yo == y)
                def _():
                    u_mine[j, k] = val

                @pl.when(yo != y)
                def _():
                    u_send[j, k] = val.astype(BF16)
        pair_copy(j).start()

    def fin_place(j, s):
        h = head0(j, y) + c * w + s * g
        return h // hn, h % hn

    def fin_copy(j, s):
        dev, off = fin_place(j, s)
        return send(
            s_out.at[j, pl.ds(s * g, g)], fin_s.at[pl.ds(off, g)],
            f_ss.at[j, s], f_rs.at[off // g], dev,
        )

    def fin_local(j, s):
        _, off = fin_place(j, s)
        return pltpu.make_async_copy(s_out.at[j, pl.ds(s * g, g)], fin_s.at[pl.ds(off, g)], f_ls)

    def chain(j):
        pair_copy(j).wait_recv()

        @pl.when(plane > 0)
        def _():
            z_copy(j).wait_recv()

        for k in range(w):
            at = pl.ds(j * w + k, 1)
            chip = fac_chip[c, y, at, :]
            other_chip = fac_pair[at, :]
            f01 = jnp.where(y == 0, chip, other_chip)
            f23 = jnp.where(y == 0, other_chip, chip)
            mine = u_mine[j, k]
            other = u_pair[j, k].astype(F32)
            entry = s_in[j, k].astype(F32)
            mid = f01 * entry + jnp.where(y == 0, mine, other)
            s_out[j, k] = (f23 * mid + jnp.where(y == 0, other, mine)).astype(BF16)
            e_send[j, k] = jnp.where(y == 0, mid, entry).astype(BF16)
            e_half[j, y, k] = jnp.where(y == 0, entry, mid).astype(BF16)

        @pl.when(plane < planes - 1)
        def _():
            z_copy(j).start()

        @pl.when(plane == planes - 1)
        def _():
            for s in range(w // g):
                dev, _off = fin_place(j, s)

                @pl.when(dev != me)
                def _():
                    fin_copy(j, s).start()

                @pl.when(dev == me)
                def _():
                    fin_local(j, s).start()
                    fin_local(j, s).wait()

    def inside_wait(i):
        load(2, q_hbm, q_s, i // 2, i % 2).wait()
        load(3, g_hbm, g_s, i // 2, i % 2).wait()

    def inside(i):
        j = i // 2
        yh = i % 2
        h0 = head0(j, yh)
        blk = tok // 2
        cols = pltpu.roll(cum_s[...], (D - h0) % D, 1)
        for hh in range(half):
            at = hcol(j, yh, hh)
            row = cumt_s[pl.ds(h0 + hh, 1), :]
            kt = kt_s[h0 + hh]
            ci = cols[:, hh:hh + 1]
            top = dot(q_s[:blk, at], kt[:, :blk], ((1,), (0,)))
            bot = dot(q_s[blk:, at], kt, ((1,), (0,)))
            top = (top * jnp.exp2((ci[:blk] - row[:, :blk]) + pen_s[:blk, :blk])).astype(BF16)
            bot = (bot * jnp.exp2((ci[blk:] - row) + pen_s[blk:, :])).astype(BF16)
            top = jnp.concatenate([top, jnp.zeros_like(top)], axis=1)
            wt = jnp.concatenate([top, bot], axis=0)
            mix_s[:, at] = dot(wt, v_s[:, at], ((1,), (0,)))
            hg = 0.5 * gain_s[:, at]
            gate_s[:, at] = hg * jnp.tanh(0.5 * g_s[:, at].astype(F32)) + hg

    def spread(j):
        e_copy(j).wait_recv()
        for yo in range(2):
            for k in range(w):
                at = pl.ds(j * w + k, 1)
                f0 = jnp.where(c == 0, fac_own[c, yo, at, :], fac_core[c, yo, at, :])
                first = e_half[j, yo, k]
                u0 = jnp.where(c == 0, u_own[j, 0, yo, k], u_core[j, yo, k]).astype(F32)
                second = (f0 * first.astype(F32) + u0).astype(BF16)
                ent[j, c, yo, k] = jnp.where(c == 0, first, second)
                x_send[j, yo, k] = jnp.where(c == 0, second, first)
        x_copy(j).start()

    def across(j):
        core_copy(j).wait_send()
        pair_copy(j).wait_send()
        e_copy(j).wait_send()

        @pl.when(plane < planes - 1)
        def _():
            z_copy(j).wait_send()

        @pl.when(plane == planes - 1)
        def _():
            for s in range(w // g):
                dev, _off = fin_place(j, s)

                @pl.when(dev != me)
                def _():
                    fin_copy(j, s).wait_send()

        x_copy(j).wait_recv()
        x_copy(j).wait_send()
        cols = pltpu.roll(lead_s[...], (D - head0(j, 0)) % D, 1)
        for yh in range(2):
            acc = ssq_s[...]
            for hh in range(half):
                at = hcol(j, yh, hh)
                lane = yh * span + hh
                st = ent[j, hh // w, yh, hh % w]
                mixed = mix_s[:, at] + cols[:, lane:lane + 1] * dot(q_s[:, at], st, ((1,), (0,)))
                acc = acc + mixed * mixed
                out_s[:, at] = (mixed * gate_s[:, at]).astype(BF16)
            ssq_s[...] = acc

    updates(0)
    update_math(0)
    own_f = jnp.where(last == before, 1.0, 0.0).astype(F32) * jnp.exp(jnp.broadcast_to(total, (heads, D)))
    for j in range(chunks):
        for yh in range(2):
            for cc in range(2):
                h = head0(j, yh) + cc * w
                fac_own[cc, yh, j * w:(j + 1) * w, :] = own_f[h:h + w]

    @pl.when(plane < planes - 1)
    def _():
        pl.semaphore_wait(barrier, GROUP)

    @pl.when(plane == planes - 1)
    def _():
        pl.semaphore_wait(barrier, GROUP - 1)

    core_copy(0).start()
    fac_core_copy().start()
    updates(1)
    update_math(1)
    core_copy(1).start()
    fac_core_copy().wait_recv()
    combine(0)
    fac_chip[...] = fac_own[...] * fac_core[...]
    fac_pair_copy().start()

    rows = lax.broadcasted_iota(jnp.int32, (tok, D), 0)
    doc_col = jnp.zeros((tok, D), jnp.int32)
    end = jnp.int32(0)
    for d in range(n_docs):
        end = end + docs_s[d]
        doc_col = doc_col + jnp.where(rows + base >= end, 1, 0)
    pen_s[...] = jnp.where(causal & (doc_col[:, :1] == doc_row), 0.0, -1e30).astype(F32)
    tri = jnp.where(causal, 1.0, 0.0).astype(BF16)
    cum = dot(tri, ld_s[...], ((1,), (1,)))
    cum_s[...] = LOG2E * cum
    lead_s[...] = jnp.where(doc_col == before, 1.0, 0.0).astype(F32) * jnp.exp(cum)
    ssq_s[...] = jnp.zeros_like(ssq_s)

    @pl.when(plane == 0)
    def _():
        s_in[...] = jnp.zeros_like(s_in)

    gain_copy.wait()
    fac_pair_copy().wait_recv()

    chain_lag = CHAIN_LAG + HOP_LAG * plane
    e_lag = jnp.maximum(chain_lag, chunks)
    spread_lag = e_lag + E_LAG
    across_lag = spread_lag + X_LAG
    steps = jnp.maximum(chunks + across_lag, 2 * chunks + 2)

    def step(t, carry):
        def at(lag, count, body):
            @pl.when((t >= lag) & (t < lag + count))
            def _():
                body(t - lag)

        at(1, chunks, combine)
        at(chain_lag, chunks, chain)
        at(e_lag, chunks, lambda j: e_copy(j).start())
        at(spread_lag, chunks, spread)

        @pl.when(t < chunks)
        def _():
            updates(t)
            inside_wait(t - 2)
            update_math(t)
            inside(t - 2)
            core_copy(t).start()

        @pl.when((t >= chunks) & (t < 2 * chunks + 2))
        def _():
            inside_wait(t - 2)
            inside(t - 2)

        at(across_lag, chunks, across)
        return carry

    lax.fori_loop(2, steps, step, 0)

    mean = jnp.sum(ssq_s[...], axis=1, keepdims=True) * (1.0 / (heads * D))
    ssq_s[...] = jnp.broadcast_to(lax.rsqrt(mean + EPS), (tok, D))

    for s in range(hn // g):
        h = me * hn + s * g
        src = (planes - 1) * GROUP + ((h // span) % 2) * 2 + (h % half) // w

        @pl.when(src != me)
        def _():
            send(
                s_out.at[0, pl.ds(0, g)], fin_s.at[pl.ds(s * g, g)], f_ss.at[0, 0], f_rs.at[s], core_peer
            ).wait_recv()

    fac_core_copy().wait_send()
    fac_pair_copy().wait_send()


def finish_kernel(mix_ref, inv_ref, fin_in, out_hbm, fin_ref, buf, sem):
    parts = buf.shape[0]
    rows = buf.shape[1]
    copies = []
    for p in range(parts):
        at = slice(p * rows, (p + 1) * rows)
        inv = inv_ref[at, :]
        for t in range(mix_ref.shape[1] // D):
            cols = slice(t * D, (t + 1) * D)
            buf[p, :, cols] = (mix_ref[at, cols].astype(F32) * inv).astype(BF16)
        copy = pltpu.make_async_copy(buf.at[p], out_hbm.at[pl.ds(p * rows, rows)], sem.at[p])
        copy.start()
        copies.append(copy)
    fin_ref[...] = fin_in[...].astype(F32)
    for copy in copies:
        copy.wait()


def shards(n, queries, keys_in, values_in, log_decay, gate_logits, norm_gain, doc_lengths):
    tok, width = queries.shape
    heads = width // D
    chunks = CHUNKS
    hc = heads // chunks
    half = hc // 2
    w = half // 2
    hn = heads // n
    g = math.gcd(w, hn)
    vm = pltpu.VMEM
    dma = pltpu.SemaphoreType.DMA
    anyspace = pl.BlockSpec(memory_space=pl.ANY)
    vspec = pl.BlockSpec(memory_space=pltpu.VMEM)
    part = vm((chunks, w, D, D), BF16)
    fac = vm((2, 2, chunks * w, D), F32)
    scratch = [
        vm((tok, width), F32), vm((tok, width), F32),
        vm((tok, width), BF16), vm((tok, width), BF16), vm((tok, width), BF16), vm((tok, width), BF16),
        vm((heads, D, tok), BF16), vm((max(heads, D), tok), BF16), vm((1, width), F32),
        pltpu.SMEM(doc_lengths.shape, jnp.int32),
        vm((tok, tok), F32), vm((heads, tok), F32), vm((heads, tok), F32), vm((tok, D), F32), vm((tok, D), F32),
        fac, fac, fac, vm((chunks * w, D), F32),
        vm((chunks, 2, 2, w, D, D), BF16), vm((chunks, 2, w, D, D), BF16), vm((chunks, w, D, D), F32),
        part, part, part, part, part,
        vm((chunks, 2, w, D, D), BF16), vm((chunks, 2, w, D, D), BF16),
        vm((chunks, 2, 2, w, D, D), BF16),
        dma((4, chunks, 2)), dma((3,)), dma((2,)), dma((2,)),
        dma((chunks,)), dma((chunks,)), dma((chunks,)), dma((chunks,)), dma((chunks,)), dma((chunks,)),
        dma((chunks,)), dma((chunks,)), dma((chunks,)), dma((chunks,)),
        dma((chunks, w // g)), dma((hn // g,)), dma,
    ]
    mixed, squares, final = pl.pallas_call(
        functools.partial(kernel, n, heads, chunks),
        out_shape=(
            pltpu.VMEM((tok, width), BF16),
            pltpu.VMEM((tok, D), F32),
            pltpu.VMEM((hn, D, D), BF16),
        ),
        in_specs=[anyspace] * 7,
        out_specs=(vspec, vspec, vspec),
        scratch_shapes=scratch,
        compiler_params=pltpu.CompilerParams(
            collective_id=0, has_side_effects=True, vmem_limit_bytes=54 * 1024 * 1024
        ),
    )(queries, keys_in, values_in, gate_logits, log_decay.T, norm_gain.reshape(1, width), doc_lengths)
    rows = tok // FINISH_PARTS
    return pl.pallas_call(
        finish_kernel,
        out_shape=(
            jax.ShapeDtypeStruct((tok, width), BF16),
            jax.ShapeDtypeStruct((hn, D, D), F32),
        ),
        in_specs=[vspec, vspec, vspec],
        out_specs=(anyspace, vspec),
        scratch_shapes=[vm((FINISH_PARTS, rows, width), BF16), dma((FINISH_PARTS,))],
        compiler_params=pltpu.CompilerParams(vmem_limit_bytes=16 * 1024 * 1024),
    )(mixed, squares, final)


def solution(mesh):
    rows = P(("grp", "seq"), None)
    return jax.shard_map(
        functools.partial(shards, mesh.shape["seq"]),
        mesh=mesh,
        in_specs=(rows, rows, rows, rows, rows, P(), P("grp")),
        out_specs=(rows, P(("grp", "seq"), None, None)),
        check_vma=False,
    )
```

```python
import functools
import math

import jax
import jax.numpy as jnp
from jax import lax
from jax.experimental import pallas as pl
from jax.experimental.pallas import tpu as pltpu
from jax.sharding import PartitionSpec as P

EPS = 1e-05
LOG2E = 1.4426950408889634
D = 128
GROUP = 4
CHUNKS = 8
CHAIN_LAG = 4
HOP_LAG = 2
E_LAG = 4
X_LAG = 2
FINISH_PARTS = 8
F32, BF16 = jnp.float32, jnp.bfloat16
MESH = pl.DeviceIdType.MESH


def dot(a, b, dims):
    return lax.dot_general(a, b, (dims, ((), ())), preferred_element_type=F32)


def kernel(
    n, heads, chunks,
    q_hbm, k_hbm, v_hbm, g_hbm, ld_hbm, gain_hbm, docs_hbm,
    out_s, ssq_s, fin_s,
    mix_s, gate_s, q_s, k_s, v_s, g_s, kt_s, ld_s, gain_s, docs_s, pen_s, cumt_s, kwt_s, cum_s, lead_s,
    fac_own, fac_core, fac_chip, fac_pair, u_own, u_core, u_mine, u_send, u_pair, s_in, s_out, e_send, e_half,
    x_send, ent,
    load_sem, small_sem, fac_ss, fac_rs, core_ss, core_rs, pair_ss, pair_rs, z_ss, z_rs, e_ss, e_rs,
    x_ss, x_rs, f_ss, f_rs, f_ls,
):
    tok = q_hbm.shape[0]
    hc = heads // chunks
    half = hc // 2
    w = half // 2
    planes = n // GROUP
    hn = heads // n
    g = math.gcd(w, hn)
    span = 2 * hn
    m = span // half
    me = lax.axis_index("seq")
    plane = me // GROUP
    r = me % GROUP
    y = r // 2
    c = r % 2
    core_peer = plane * GROUP + y * 2 + (1 - c)
    pair_peer = plane * GROUP + (1 - y) * 2 + c

    def send(src, dst, ss, rs, dev):
        return pltpu.make_async_remote_copy(
            src_ref=src, dst_ref=dst, send_sem=ss, recv_sem=rs,
            device_id={"seq": dev}, device_id_type=MESH,
        )

    def head0(j, yh):
        return (j // m) * (2 * span) + yh * span + (j % m) * half

    def hcols(j, yh):
        return pl.ds(pl.multiple_of(head0(j, yh) * D, half * D), half * D)

    def hcol(j, yh, hh):
        return pl.ds(pl.multiple_of((head0(j, yh) + hh) * D, D), D)

    def load(which, hbm, vm, j, yh):
        at = hcols(j, yh)
        return pltpu.make_async_copy(hbm.at[:, at], vm.at[:, at], load_sem.at[which, j, yh])

    def start_pair(a, a_hbm, a_vm, b, b_hbm, b_vm):
        def go(j, carry):
            for yh in range(2):
                load(a, a_hbm, a_vm, j, yh).start()
                load(b, b_hbm, b_vm, j, yh).start()
            return carry
        return go

    ld_copy = pltpu.make_async_copy(ld_hbm, ld_s.at[pl.ds(0, heads)], small_sem.at[0])
    docs_copy = pltpu.make_async_copy(docs_hbm, docs_s, small_sem.at[1])
    gain_copy = pltpu.make_async_copy(gain_hbm, gain_s, small_sem.at[2])
    ld_copy.start()
    docs_copy.start()
    lax.fori_loop(0, chunks, start_pair(0, k_hbm, k_s, 1, v_hbm, v_s), 0)

    barrier = pltpu.get_barrier_semaphore()
    for d in range(1, GROUP):
        pl.semaphore_signal(
            barrier, inc=1, device_id={"seq": plane * GROUP + (r + d) % GROUP}, device_id_type=MESH
        )

    @pl.when(plane > 0)
    def _():
        pl.semaphore_signal(barrier, inc=1, device_id={"seq": me - GROUP}, device_id_type=MESH)

    gain_copy.start()
    lax.fori_loop(0, chunks, start_pair(2, q_hbm, q_s, 3, g_hbm, g_s), 0)

    if heads < D:
        ld_s[pl.ds(heads, D - heads)] = jnp.zeros((D - heads, tok), BF16)
    base = me * tok
    row_i = lax.broadcasted_iota(jnp.int32, (tok, tok), 0)
    col_i = lax.broadcasted_iota(jnp.int32, (tok, tok), 1)
    causal = row_i >= col_i
    lanes = lax.broadcasted_iota(jnp.int32, (1, tok), 1)
    docs_copy.wait()
    n_docs = docs_s.shape[0]
    doc_row = jnp.zeros((1, tok), jnp.int32)
    before = jnp.int32(0)
    last = jnp.int32(0)
    end = jnp.int32(0)
    for d in range(n_docs):
        end = end + docs_s[d]
        doc_row = doc_row + jnp.where(lanes + base >= end, 1, 0)
        before = before + jnp.where(base - 1 >= end, 1, 0)
        last = last + jnp.where(base + tok - 1 >= end, 1, 0)
    closing = jnp.where(doc_row == last, 1.0, 0.0).astype(F32)
    ld_copy.wait()
    upper = jnp.where(row_i <= col_i, 1.0, 0.0).astype(BF16)
    cumt = dot(ld_s[pl.ds(0, heads)], upper, ((1,), (0,)))
    cumt_s[...] = LOG2E * cumt
    total = cumt[:, tok - 1:tok]
    kwt_s[...] = closing * jnp.exp(total - cumt)

    def updates(j):
        for yh in range(2):
            load(0, k_hbm, k_s, j, yh).wait()
            load(1, v_hbm, v_s, j, yh).wait()

    def update_math(j):
        for yh in range(2):
            for hh in range(half):
                h = head0(j, yh) + hh
                kt = k_s[:, hcol(j, yh, hh)].T
                kt_s[h] = kt
                wk = (kt.astype(F32) * kwt_s[pl.ds(h, 1), :]).astype(BF16)
                up = dot(wk, v_s[:, hcol(j, yh, hh)], ((1,), (0,)))
                u_own[j, hh // w, yh, hh % w] = up.astype(BF16)

    def core_copy(j):
        return send(u_own.at[j, 1 - c], u_core.at[j], core_ss.at[j], core_rs.at[j], core_peer)

    def pair_copy(j):
        return send(u_send.at[j], u_pair.at[j], pair_ss.at[j], pair_rs.at[j], pair_peer)

    def z_copy(j):
        return send(s_out.at[j], s_in.at[j], z_ss.at[j], z_rs.at[j], (me + GROUP) % n)

    def e_copy(j):
        return send(e_send.at[j], e_half.at[j, y], e_ss.at[j], e_rs.at[j], pair_peer)

    def x_copy(j):
        return send(x_send.at[j], ent.at[j, c], x_ss.at[j], x_rs.at[j], core_peer)

    def fac_core_copy():
        return send(fac_own, fac_core, fac_ss.at[0], fac_rs.at[0], core_peer)

    def fac_pair_copy():
        return send(fac_chip.at[c, 1 - y], fac_pair, fac_ss.at[1], fac_rs.at[1], pair_peer)

    def combine(j):
        core_copy(j).wait_recv()
        for k in range(w):
            for yo in range(2):
                at = pl.ds(j * w + k, 1)
                fa = jnp.where(c == 0, fac_core[c, yo, at, :], 1.0)
                fb = jnp.where(c == 0, 1.0, fac_own[c, yo, at, :])
                val = fa * u_own[j, c, yo, k].astype(F32) + fb * u_core[j, yo, k].astype(F32)

                @pl.when(yo == y)
                def _():
                    u_mine[j, k] = val

                @pl.when(yo != y)
                def _():
                    u_send[j, k] = val.astype(BF16)
        pair_copy(j).start()

    def fin_place(j, s):
        h = head0(j, y) + c * w + s * g
        return h // hn, h % hn

    def fin_copy(j, s):
        dev, off = fin_place(j, s)
        return send(
            s_out.at[j, pl.ds(s * g, g)], fin_s.at[pl.ds(off, g)],
            f_ss.at[j, s], f_rs.at[off // g], dev,
        )

    def fin_local(j, s):
        _, off = fin_place(j, s)
        return pltpu.make_async_copy(s_out.at[j, pl.ds(s * g, g)], fin_s.at[pl.ds(off, g)], f_ls)

    def chain(j):
        @pl.when(j == 0)
        def _():
            fac_pair_copy().wait_recv()

        pair_copy(j).wait_recv()

        @pl.when(plane > 0)
        def _():
            z_copy(j).wait_recv()

        for k in range(w):
            at = pl.ds(j * w + k, 1)
            chip = fac_chip[c, y, at, :]
            other_chip = fac_pair[at, :]
            f01 = jnp.where(y == 0, chip, other_chip)
            f23 = jnp.where(y == 0, other_chip, chip)
            mine = u_mine[j, k]
            other = u_pair[j, k].astype(F32)
            entry = s_in[j, k].astype(F32)
            mid = f01 * entry + jnp.where(y == 0, mine, other)
            s_out[j, k] = (f23 * mid + jnp.where(y == 0, other, mine)).astype(BF16)
            e_send[j, k] = jnp.where(y == 0, mid, entry).astype(BF16)
            e_half[j, y, k] = jnp.where(y == 0, entry, mid).astype(BF16)

        @pl.when(plane < planes - 1)
        def _():
            z_copy(j).start()

        @pl.when(plane == planes - 1)
        def _():
            for s in range(w // g):
                dev, _off = fin_place(j, s)

                @pl.when(dev != me)
                def _():
                    fin_copy(j, s).start()

                @pl.when(dev == me)
                def _():
                    fin_local(j, s).start()
                    fin_local(j, s).wait()

    def inside_wait(i):
        load(2, q_hbm, q_s, i // 2, i % 2).wait()
        load(3, g_hbm, g_s, i // 2, i % 2).wait()

    def inside(i):
        j = i // 2
        yh = i % 2
        h0 = head0(j, yh)
        blk = tok // 2
        cols = pltpu.roll(cum_s[...], (D - h0) % D, 1)
        for hh in range(half):
            at = hcol(j, yh, hh)
            row = cumt_s[pl.ds(h0 + hh, 1), :]
            kt = kt_s[h0 + hh]
            ci = cols[:, hh:hh + 1]
            top = dot(q_s[:blk, at], kt[:, :blk], ((1,), (0,)))
            bot = dot(q_s[blk:, at], kt, ((1,), (0,)))
            top = (top * jnp.exp2((ci[:blk] - row[:, :blk]) + pen_s[:blk, :blk])).astype(BF16)
            bot = (bot * jnp.exp2((ci[blk:] - row) + pen_s[blk:, :])).astype(BF16)
            top = jnp.concatenate([top, jnp.zeros_like(top)], axis=1)
            wt = jnp.concatenate([top, bot], axis=0)
            mix_s[:, at] = dot(wt, v_s[:, at], ((1,), (0,)))
            hg = 0.5 * gain_s[:, at]
            gate_s[:, at] = hg * jnp.tanh(0.5 * g_s[:, at].astype(F32)) + hg

    def spread(j):
        e_copy(j).wait_recv()
        for yo in range(2):
            for k in range(w):
                at = pl.ds(j * w + k, 1)
                f0 = jnp.where(c == 0, fac_own[c, yo, at, :], fac_core[c, yo, at, :])
                first = e_half[j, yo, k]
                u0 = jnp.where(c == 0, u_own[j, 0, yo, k], u_core[j, yo, k]).astype(F32)
                second = (f0 * first.astype(F32) + u0).astype(BF16)
                ent[j, c, yo, k] = jnp.where(c == 0, first, second)
                x_send[j, yo, k] = jnp.where(c == 0, second, first)
        x_copy(j).start()

    def across(j):
        core_copy(j).wait_send()
        pair_copy(j).wait_send()
        e_copy(j).wait_send()

        @pl.when(plane < planes - 1)
        def _():
            z_copy(j).wait_send()

        @pl.when(plane == planes - 1)
        def _():
            for s in range(w // g):
                dev, _off = fin_place(j, s)

                @pl.when(dev != me)
                def _():
                    fin_copy(j, s).wait_send()

        x_copy(j).wait_recv()
        x_copy(j).wait_send()
        cols = pltpu.roll(lead_s[...], (D - head0(j, 0)) % D, 1)
        for yh in range(2):
            acc = ssq_s[...]
            for hh in range(half):
                at = hcol(j, yh, hh)
                lane = yh * span + hh
                st = ent[j, hh // w, yh, hh % w]
                mixed = mix_s[:, at] + cols[:, lane:lane + 1] * dot(q_s[:, at], st, ((1,), (0,)))
                acc = acc + mixed * mixed
                out_s[:, at] = (mixed * gate_s[:, at]).astype(BF16)
            ssq_s[...] = acc

    updates(0)
    update_math(0)
    own_f = jnp.where(last == before, 1.0, 0.0).astype(F32) * jnp.exp(jnp.broadcast_to(total, (heads, D)))
    for j in range(chunks):
        for yh in range(2):
            for cc in range(2):
                h = head0(j, yh) + cc * w
                fac_own[cc, yh, j * w:(j + 1) * w, :] = own_f[h:h + w]

    @pl.when(plane < planes - 1)
    def _():
        pl.semaphore_wait(barrier, GROUP)

    @pl.when(plane == planes - 1)
    def _():
        pl.semaphore_wait(barrier, GROUP - 1)

    core_copy(0).start()
    fac_core_copy().start()
    updates(1)
    update_math(1)
    core_copy(1).start()
    rows = lax.broadcasted_iota(jnp.int32, (tok, D), 0)
    doc_col = jnp.zeros((tok, D), jnp.int32)
    end = jnp.int32(0)
    for d in range(n_docs):
        end = end + docs_s[d]
        doc_col = doc_col + jnp.where(rows + base >= end, 1, 0)
    pen_s[...] = jnp.where(causal & (doc_col[:, :1] == doc_row), 0.0, -1e30).astype(F32)
    tri = jnp.where(causal, 1.0, 0.0).astype(BF16)
    cum = dot(tri, ld_s[...], ((1,), (1,)))
    cum_s[...] = LOG2E * cum
    lead_s[...] = jnp.where(doc_col == before, 1.0, 0.0).astype(F32) * jnp.exp(cum)
    ssq_s[...] = jnp.zeros_like(ssq_s)

    @pl.when(plane == 0)
    def _():
        s_in[...] = jnp.zeros_like(s_in)

    gain_copy.wait()
    fac_core_copy().wait_recv()
    fac_chip[...] = fac_own[...] * fac_core[...]
    fac_pair_copy().start()

    chain_lag = CHAIN_LAG + HOP_LAG * plane
    e_lag = jnp.maximum(chain_lag, chunks + 2)
    spread_lag = e_lag + E_LAG
    across_lag = spread_lag + X_LAG
    steps = jnp.maximum(chunks + across_lag, 2 * chunks + 2)

    def step(t, carry):
        def at(lag, count, body):
            @pl.when((t >= lag) & (t < lag + count))
            def _():
                body(t - lag)

        at(2, chunks, combine)
        at(chain_lag, chunks, chain)
        at(e_lag, chunks, lambda j: e_copy(j).start())
        at(spread_lag, chunks, spread)

        @pl.when(t < chunks)
        def _():
            updates(t)
            inside_wait(t - 2)
            update_math(t)
            inside(t - 2)
            core_copy(t).start()

        @pl.when((t >= chunks) & (t < 2 * chunks + 2))
        def _():
            inside_wait(t - 2)
            inside(t - 2)

        at(across_lag, chunks, across)
        return carry

    lax.fori_loop(2, steps, step, 0)

    mean = jnp.sum(ssq_s[...], axis=1, keepdims=True) * (1.0 / (heads * D))
    ssq_s[...] = jnp.broadcast_to(lax.rsqrt(mean + EPS), (tok, D))

    for s in range(hn // g):
        h = me * hn + s * g
        src = (planes - 1) * GROUP + ((h // span) % 2) * 2 + (h % half) // w

        @pl.when(src != me)
        def _():
            send(
                s_out.at[0, pl.ds(0, g)], fin_s.at[pl.ds(s * g, g)], f_ss.at[0, 0], f_rs.at[s], core_peer
            ).wait_recv()

    fac_core_copy().wait_send()
    fac_pair_copy().wait_send()


def finish_kernel(mix_ref, inv_ref, fin_in, out_hbm, fin_ref, buf, sem):
    parts = buf.shape[0]
    rows = buf.shape[1]
    copies = []
    for p in range(parts):
        at = slice(p * rows, (p + 1) * rows)
        inv = inv_ref[at, :]
        for t in range(mix_ref.shape[1] // D):
            cols = slice(t * D, (t + 1) * D)
            buf[p, :, cols] = (mix_ref[at, cols].astype(F32) * inv).astype(BF16)
        copy = pltpu.make_async_copy(buf.at[p], out_hbm.at[pl.ds(p * rows, rows)], sem.at[p])
        copy.start()
        copies.append(copy)
    fin_ref[...] = fin_in[...].astype(F32)
    for copy in copies:
        copy.wait()


def shards(n, queries, keys_in, values_in, log_decay, gate_logits, norm_gain, doc_lengths):
    tok, width = queries.shape
    heads = width // D
    chunks = CHUNKS
    hc = heads // chunks
    half = hc // 2
    w = half // 2
    hn = heads // n
    g = math.gcd(w, hn)
    vm = pltpu.VMEM
    dma = pltpu.SemaphoreType.DMA
    anyspace = pl.BlockSpec(memory_space=pl.ANY)
    vspec = pl.BlockSpec(memory_space=pltpu.VMEM)
    part = vm((chunks, w, D, D), BF16)
    fac = vm((2, 2, chunks * w, D), F32)
    scratch = [
        vm((tok, width), F32), vm((tok, width), F32),
        vm((tok, width), BF16), vm((tok, width), BF16), vm((tok, width), BF16), vm((tok, width), BF16),
        vm((heads, D, tok), BF16), vm((max(heads, D), tok), BF16), vm((1, width), F32),
        pltpu.SMEM(doc_lengths.shape, jnp.int32),
        vm((tok, tok), F32), vm((heads, tok), F32), vm((heads, tok), F32), vm((tok, D), F32), vm((tok, D), F32),
        fac, fac, fac, vm((chunks * w, D), F32),
        vm((chunks, 2, 2, w, D, D), BF16), vm((chunks, 2, w, D, D), BF16), vm((chunks, w, D, D), F32),
        part, part, part, part, part,
        vm((chunks, 2, w, D, D), BF16), vm((chunks, 2, w, D, D), BF16),
        vm((chunks, 2, 2, w, D, D), BF16),
        dma((4, chunks, 2)), dma((3,)), dma((2,)), dma((2,)),
        dma((chunks,)), dma((chunks,)), dma((chunks,)), dma((chunks,)), dma((chunks,)), dma((chunks,)),
        dma((chunks,)), dma((chunks,)), dma((chunks,)), dma((chunks,)),
        dma((chunks, w // g)), dma((hn // g,)), dma,
    ]
    mixed, squares, final = pl.pallas_call(
        functools.partial(kernel, n, heads, chunks),
        out_shape=(
            pltpu.VMEM((tok, width), BF16),
            pltpu.VMEM((tok, D), F32),
            pltpu.VMEM((hn, D, D), BF16),
        ),
        in_specs=[anyspace] * 7,
        out_specs=(vspec, vspec, vspec),
        scratch_shapes=scratch,
        compiler_params=pltpu.CompilerParams(
            collective_id=0, has_side_effects=True, vmem_limit_bytes=54 * 1024 * 1024
        ),
    )(queries, keys_in, values_in, gate_logits, log_decay.T, norm_gain.reshape(1, width), doc_lengths)
    rows = tok // FINISH_PARTS
    return pl.pallas_call(
        finish_kernel,
        out_shape=(
            jax.ShapeDtypeStruct((tok, width), BF16),
            jax.ShapeDtypeStruct((hn, D, D), F32),
        ),
        in_specs=[vspec, vspec, vspec],
        out_specs=(anyspace, vspec),
        scratch_shapes=[vm((FINISH_PARTS, rows, width), BF16), dma((FINISH_PARTS,))],
        compiler_params=pltpu.CompilerParams(vmem_limit_bytes=16 * 1024 * 1024),
    )(mixed, squares, final)


def solution(mesh):
    rows = P(("grp", "seq"), None)
    return jax.shard_map(
        functools.partial(shards, mesh.shape["seq"]),
        mesh=mesh,
        in_specs=(rows, rows, rows, rows, rows, P(), P("grp")),
        out_specs=(rows, P(("grp", "seq"), None, None)),
        check_vma=False,
    )
```

```python
import functools
import math

import jax
import jax.numpy as jnp
from jax import lax
from jax.experimental import pallas as pl
from jax.experimental.pallas import tpu as pltpu
from jax.sharding import PartitionSpec as P

EPS = 1e-05
LOG2E = 1.4426950408889634
D = 128
GROUP = 4
CHUNKS = 16
LOADS = 8
CHAIN_LAG = 9
HOP_LAG = 4
E_LAG = 5
X_LAG = 2
FINISH_PARTS = 8
F32, BF16 = jnp.float32, jnp.bfloat16
MESH = pl.DeviceIdType.MESH


def dot(a, b, dims):
    return lax.dot_general(a, b, (dims, ((), ())), preferred_element_type=F32)


def kernel(
    n, heads, chunks,
    q_hbm, k_hbm, v_hbm, g_hbm, ld_hbm, gain_hbm, docs_hbm,
    out_s, ssq_s, fin_s,
    mix_s, gate_s, kv_s, qg_s, kt_s, ld_s, gain_s, docs_s, pen_s, cumt_s, kwt_s, cum_s, lead_s,
    fac_own, fac_core, fac_chip, fac_pair, wt_s, u_own, u_core, u_mine, u_send, u_pair, s_in, s_out, e_send, e_half,
    x_send, ent,
    kv_sem, qg_sem, small_sem, fac_ss, fac_rs, core_ss, core_rs, pair_ss, pair_rs, z_ss, z_rs, e_ss, e_rs,
    x_ss, x_rs, f_ss, f_rs, f_ls,
):
    tok = q_hbm.shape[0]
    hc = heads // chunks
    half = hc // 2
    w = half // 2
    planes = n // GROUP
    loads = LOADS
    per = chunks // loads
    hn = heads // n
    g = math.gcd(w, hn)
    span = 2 * hn
    m = span // half
    me = lax.axis_index("seq")
    plane = me // GROUP
    r = me % GROUP
    y = r // 2
    c = r % 2
    core_peer = plane * GROUP + y * 2 + (1 - c)
    pair_peer = plane * GROUP + (1 - y) * 2 + c

    def send(src, dst, ss, rs, dev):
        return pltpu.make_async_remote_copy(
            src_ref=src, dst_ref=dst, send_sem=ss, recv_sem=rs,
            device_id={"seq": dev}, device_id_type=MESH,
        )

    def head0(j, yh):
        return (j // m) * (2 * span) + yh * span + (j % m) * half

    def hcol(j, yh, hh):
        return pl.ds(pl.multiple_of((head0(j, yh) + hh) * D, D), D)

    k_s, v_s = kv_s.at[0], kv_s.at[1]
    q_s, g_s = qg_s.at[0], qg_s.at[1]

    def fetch(first, second, both, sem):
        def go(p, carry):
            for yh in range(2):
                at = pl.ds(pl.multiple_of(head0(p * per, yh) * D, half * per * D), half * per * D)
                pltpu.make_async_copy(first.at[:, at], both.at[0, :, at], sem.at[p]).start()
                pltpu.make_async_copy(second.at[:, at], both.at[1, :, at], sem.at[p]).start()
            return carry
        return go

    def fetched(both, sem, p):
        part = both.at[:, :, pl.ds(0, 2 * half * per * D)]
        pltpu.make_async_copy(part, part, sem.at[p]).wait()

    barrier = pltpu.get_barrier_semaphore()
    for d in range(1, GROUP):
        pl.semaphore_signal(
            barrier, inc=1, device_id={"seq": plane * GROUP + (r + d) % GROUP}, device_id_type=MESH
        )

    @pl.when(plane > 0)
    def _():
        pl.semaphore_signal(barrier, inc=1, device_id={"seq": me - GROUP}, device_id_type=MESH)

    ld_copy = pltpu.make_async_copy(ld_hbm, ld_s.at[pl.ds(0, heads)], small_sem.at[0])
    docs_copy = pltpu.make_async_copy(docs_hbm, docs_s, small_sem.at[1])
    gain_copy = pltpu.make_async_copy(gain_hbm, gain_s, small_sem.at[2])
    ld_copy.start()
    docs_copy.start()
    lax.fori_loop(0, loads, fetch(k_hbm, v_hbm, kv_s, kv_sem), 0)

    gain_copy.start()
    lax.fori_loop(0, loads, fetch(q_hbm, g_hbm, qg_s, qg_sem), 0)

    if heads < D:
        ld_s[pl.ds(heads, D - heads)] = jnp.zeros((D - heads, tok), BF16)
    base = me * tok
    row_i = lax.broadcasted_iota(jnp.int32, (tok, tok), 0)
    col_i = lax.broadcasted_iota(jnp.int32, (tok, tok), 1)
    causal = row_i >= col_i
    lanes = lax.broadcasted_iota(jnp.int32, (1, tok), 1)
    docs_copy.wait()
    n_docs = docs_s.shape[0]
    doc_row = jnp.zeros((1, tok), jnp.int32)
    before = jnp.int32(0)
    last = jnp.int32(0)
    end = jnp.int32(0)
    for d in range(n_docs):
        end = end + docs_s[d]
        doc_row = doc_row + jnp.where(lanes + base >= end, 1, 0)
        before = before + jnp.where(base - 1 >= end, 1, 0)
        last = last + jnp.where(base + tok - 1 >= end, 1, 0)
    closing = jnp.where(doc_row == last, 1.0, 0.0).astype(F32)
    ld_copy.wait()
    upper = jnp.where(row_i <= col_i, 1.0, 0.0).astype(BF16)
    cumt = dot(ld_s[pl.ds(0, heads)], upper, ((1,), (0,)))
    cumt_s[...] = LOG2E * cumt
    total = cumt[:, tok - 1:tok]
    kwt_s[...] = closing * jnp.exp(total - cumt)

    def updates(u):
        fetched(kv_s, kv_sem, u)

    def update_math(j):
        for yh in range(2):
            for hh in range(half):
                h = head0(j, yh) + hh
                kt = k_s[:, hcol(j, yh, hh)].T
                kt_s[h] = kt
                wk = (kt.astype(F32) * kwt_s[pl.ds(h, 1), :]).astype(BF16)
                up = dot(wk, v_s[:, hcol(j, yh, hh)], ((1,), (0,)))
                u_own[j, hh // w, yh, hh % w] = up.astype(BF16)

    def core_copy(j):
        return send(u_own.at[j, 1 - c], u_core.at[j], core_ss, core_rs.at[j], core_peer)

    def pair_copy(j):
        return send(u_send.at[j], u_pair.at[j], pair_ss, pair_rs.at[j], pair_peer)

    def z_copy(j):
        return send(s_out.at[j], s_in.at[j], z_ss, z_rs.at[j], (me + GROUP) % n)

    def e_copy(j):
        return send(e_send.at[j], e_half.at[j, y], e_ss, e_rs.at[j], pair_peer)

    def x_copy(j):
        return send(x_send.at[j], ent.at[j, c], x_ss, x_rs.at[j], core_peer)

    def fac_core_copy():
        return send(fac_own, fac_core, fac_ss.at[0], fac_rs.at[0], core_peer)

    def fac_pair_copy():
        return send(fac_chip.at[c, 1 - y], fac_pair, fac_ss.at[1], fac_rs.at[1], pair_peer)

    def combine(j):
        core_copy(j).wait_recv()
        for k in range(w):
            for yo in range(2):
                at = pl.ds(j * w + k, 1)
                fa = jnp.where(c == 0, fac_core[c, yo, at, :], 1.0)
                fb = jnp.where(c == 0, 1.0, fac_own[c, yo, at, :])
                val = fa * u_own[j, c, yo, k].astype(F32) + fb * u_core[j, yo, k].astype(F32)

                @pl.when(yo == y)
                def _():
                    u_mine[j, k] = val

                @pl.when(yo != y)
                def _():
                    u_send[j, k] = val.astype(BF16)
        pair_copy(j).start()

    def fin_place(j, s):
        h = head0(j, y) + c * w + s * g
        return h // hn, h % hn

    def fin_copy(j, s):
        dev, off = fin_place(j, s)
        return send(
            s_out.at[j, pl.ds(s * g, g)], fin_s.at[pl.ds(off, g)],
            f_ss, f_rs.at[off // g], dev,
        )

    def fin_local(j, s):
        _, off = fin_place(j, s)
        return pltpu.make_async_copy(s_out.at[j, pl.ds(s * g, g)], fin_s.at[pl.ds(off, g)], f_ls)

    def chain(j):
        @pl.when(j == 0)
        def _():
            fac_pair_copy().wait_recv()

        pair_copy(j).wait_recv()

        @pl.when(plane > 0)
        def _():
            z_copy(j).wait_recv()

        for k in range(w):
            at = pl.ds(j * w + k, 1)
            chip = fac_chip[c, y, at, :]
            other_chip = fac_pair[at, :]
            f01 = jnp.where(y == 0, chip, other_chip)
            f23 = jnp.where(y == 0, other_chip, chip)
            mine = u_mine[j, k]
            other = u_pair[j, k].astype(F32)
            entry = s_in[j, k].astype(F32)
            mid = f01 * entry + jnp.where(y == 0, mine, other)
            s_out[j, k] = (f23 * mid + jnp.where(y == 0, other, mine)).astype(BF16)
            e_send[j, k] = jnp.where(y == 0, mid, entry).astype(BF16)
            e_half[j, y, k] = jnp.where(y == 0, entry, mid).astype(BF16)

        @pl.when(plane < planes - 1)
        def _():
            z_copy(j).start()

        @pl.when(plane == planes - 1)
        def _():
            for s in range(w // g):
                dev, _off = fin_place(j, s)

                @pl.when(dev != me)
                def _():
                    fin_copy(j, s).start()

                @pl.when(dev == me)
                def _():
                    fin_local(j, s).start()
                    fin_local(j, s).wait()

    def inside_wait(i):
        @pl.when((i % 2 == 0) & (i < 2 * loads))
        def _():
            fetched(qg_s, qg_sem, i // 2)

    def place(i):
        j = (i // 2) * per
        return j, i % 2, head0(j, i % 2)

    def weigh(i):
        j, yh, h0 = place(i)
        blk = tok // 2
        cols = pltpu.roll(cum_s[...], (D - h0) % D, 1)
        for hh in range(half * per):
            at = hcol(j, yh, hh)
            row = cumt_s[pl.ds(h0 + hh, 1), :]
            kt = kt_s[h0 + hh]
            ci = cols[:, hh:hh + 1]
            top = dot(q_s[:blk, at], kt[:, :blk], ((1,), (0,)))
            bot = dot(q_s[blk:, at], kt, ((1,), (0,)))
            top = (top * jnp.exp2((ci[:blk] - row[:, :blk]) + pen_s[:blk, :blk])).astype(BF16)
            bot = (bot * jnp.exp2((ci[blk:] - row) + pen_s[blk:, :])).astype(BF16)
            wt_s[hh, :blk, :blk] = top
            wt_s[hh, blk:, :] = bot

    def apply(i):
        j, yh, h0 = place(i)
        for hh in range(half * per):
            at = hcol(j, yh, hh)
            mix_s[:, at] = dot(wt_s[hh], v_s[:, at], ((1,), (0,)))
            hg = 0.5 * gain_s[:, at]
            gate_s[:, at] = hg * jnp.tanh(0.5 * g_s[:, at].astype(F32)) + hg

    def spread(j):
        e_copy(j).wait_recv()
        for yo in range(2):
            for k in range(w):
                at = pl.ds(j * w + k, 1)
                f0 = jnp.where(c == 0, fac_own[c, yo, at, :], fac_core[c, yo, at, :])
                first = e_half[j, yo, k]
                u0 = jnp.where(c == 0, u_own[j, 0, yo, k], u_core[j, yo, k]).astype(F32)
                second = (f0 * first.astype(F32) + u0).astype(BF16)
                ent[j, c, yo, k] = jnp.where(c == 0, first, second)
                x_send[j, yo, k] = jnp.where(c == 0, second, first)
        x_copy(j).start()

    def across_wait(a):
        for b in range(per):
            x_copy(a * per + b).wait_recv()

    def across(a):
        j = a * per
        cols = pltpu.roll(lead_s[...], (D - head0(j, 0)) % D, 1)
        acc = ssq_s[...]
        for yh in range(2):
            for hh in range(half * per):
                at = hcol(j, yh, hh)
                lane = yh * span + hh
                st = ent[j + hh // half, (hh % half) // w, yh, hh % w]
                mixed = mix_s[:, at] + cols[:, lane:lane + 1] * dot(q_s[:, at], st, ((1,), (0,)))
                acc = acc + mixed * mixed
                out_s[:, at] = (mixed * gate_s[:, at]).astype(BF16)
        ssq_s[...] = acc

    updates(0)
    update_math(0)
    own_f = jnp.where(last == before, 1.0, 0.0).astype(F32) * jnp.exp(jnp.broadcast_to(total, (heads, D)))
    for j in range(chunks):
        for yh in range(2):
            for cc in range(2):
                h = head0(j, yh) + cc * w
                fac_own[cc, yh, j * w:(j + 1) * w, :] = own_f[h:h + w]

    @pl.when(plane < planes - 1)
    def _():
        pl.semaphore_wait(barrier, GROUP)

    @pl.when(plane == planes - 1)
    def _():
        pl.semaphore_wait(barrier, GROUP - 1)

    core_copy(0).start()
    fac_core_copy().start()
    for j in range(1, per):
        update_math(j)
        core_copy(j).start()
    updates(1)
    for j in range(per, 2 * per):
        update_math(j)
        core_copy(j).start()
    fac_core_copy().wait_recv()
    fac_chip[...] = fac_own[...] * fac_core[...]
    fac_pair_copy().start()
    for j in range(per):
        combine(j)

    rows = lax.broadcasted_iota(jnp.int32, (tok, D), 0)
    doc_col = jnp.zeros((tok, D), jnp.int32)
    end = jnp.int32(0)
    for d in range(n_docs):
        end = end + docs_s[d]
        doc_col = doc_col + jnp.where(rows + base >= end, 1, 0)
    pen_s[...] = jnp.where(causal & (doc_col[:, :1] == doc_row), 0.0, -1e30).astype(F32)
    tri = jnp.where(causal, 1.0, 0.0).astype(BF16)
    cum = dot(tri, ld_s[...], ((1,), (1,)))
    cum_s[...] = LOG2E * cum
    lead_s[...] = jnp.where(doc_col == before, 1.0, 0.0).astype(F32) * jnp.exp(cum)
    ssq_s[...] = jnp.zeros_like(ssq_s)

    @pl.when(plane == 0)
    def _():
        s_in[...] = jnp.zeros_like(s_in)

    gain_copy.wait()
    wt_s[...] = jnp.zeros_like(wt_s)
    for j in range(per, 2 * per):
        combine(j)
    updates(2)
    inside_wait(0)
    for j in range(2 * per, 3 * per):
        update_math(j)
    weigh(0)
    for j in range(2 * per, 3 * per):
        core_copy(j).start()

    chain_lag = CHAIN_LAG + HOP_LAG * plane
    e_lag = jnp.maximum(chain_lag, chunks + per + 1)
    spread_lag = e_lag + E_LAG
    across_lag = spread_lag + 2 + X_LAG
    steps = jnp.maximum(across_lag + chunks, (2 * loads + 3) * per)

    def step(t, carry):
        def at(lag, count, body, first=0):
            @pl.when((t >= lag + first) & (t < lag + count))
            def _():
                body(t - lag)

        at(per + 1, chunks, combine, 2 * per)
        at(chain_lag, chunks, chain)
        at(e_lag, chunks, lambda j: e_copy(j).start())
        at(spread_lag, chunks, spread)

        u = t // per
        a = (t - across_lag) // per
        even = t % per == 0
        late = even & (u >= loads) & (u < 2 * loads + 3)
        states = even & (t >= across_lag) & (t < across_lag + chunks)

        @pl.when(even & (u < loads))
        def _():
            updates(u)
            inside_wait(u - 2)
            for j in range(per):
                update_math(t + j)
            apply(u - 3)
            weigh(u - 2)
            for j in range(per):
                core_copy(t + j).start()

        @pl.when(late)
        def _():
            inside_wait(u - 2)

        @pl.when(states)
        def _():
            across_wait(a)

        @pl.when(late & states)
        def _():
            apply(u - 3)
            weigh(jnp.minimum(u - 2, 2 * loads - 1))
            across(a)

        @pl.when(late & jnp.logical_not(states))
        def _():
            apply(u - 3)
            weigh(jnp.minimum(u - 2, 2 * loads - 1))

        @pl.when(states & jnp.logical_not(late))
        def _():
            across(a)

        return carry

    lax.fori_loop(3 * per, steps, step, 0)

    mean = jnp.sum(ssq_s[...], axis=1, keepdims=True) * (1.0 / (heads * D))
    ssq_s[...] = jnp.broadcast_to(lax.rsqrt(mean + EPS), (tok, D))

    for s in range(hn // g):
        h = me * hn + s * g
        src = (planes - 1) * GROUP + ((h // span) % 2) * 2 + (h % half) // w

        @pl.when(src != me)
        def _():
            send(
                s_out.at[0, pl.ds(0, g)], fin_s.at[pl.ds(s * g, g)], f_ss, f_rs.at[s], core_peer
            ).wait_recv()

    fac_core_copy().wait_send()
    fac_pair_copy().wait_send()
    send(u_own.at[:, 1 - c], u_core, core_ss, core_rs.at[0], core_peer).wait_send()
    send(u_send, u_pair, pair_ss, pair_rs.at[0], pair_peer).wait_send()
    send(e_send, s_in, e_ss, e_rs.at[0], pair_peer).wait_send()
    send(x_send, e_half, x_ss, x_rs.at[0], core_peer).wait_send()

    @pl.when(plane < planes - 1)
    def _():
        send(s_out, s_in, z_ss, z_rs.at[0], (me + GROUP) % n).wait_send()

    @pl.when(plane == planes - 1)
    def _():
        sent = pl.ds(0, chunks - max(1, hn // (2 * w)))
        send(s_out.at[sent], s_in.at[sent], f_ss, f_rs.at[0], core_peer).wait_send()


def finish_kernel(mix_ref, inv_ref, fin_in, out_hbm, fin_hbm, buf, fin_s, sem, fin_sem):
    parts = buf.shape[0]
    rows = buf.shape[1]
    fin_s[...] = fin_in[...].astype(F32)
    fin_copy = pltpu.make_async_copy(fin_s, fin_hbm, fin_sem)
    fin_copy.start()
    copies = [fin_copy]
    for p in range(parts):
        at = slice(p * rows, (p + 1) * rows)
        inv = inv_ref[at, :]
        for t in range(mix_ref.shape[1] // D):
            cols = slice(t * D, (t + 1) * D)
            buf[p, :, cols] = (mix_ref[at, cols].astype(F32) * inv).astype(BF16)
        copy = pltpu.make_async_copy(buf.at[p], out_hbm.at[pl.ds(p * rows, rows)], sem.at[p])
        copy.start()
        copies.append(copy)
    for copy in copies:
        copy.wait()


def shards(n, queries, keys_in, values_in, log_decay, gate_logits, norm_gain, doc_lengths):
    tok, width = queries.shape
    heads = width // D
    chunks = CHUNKS
    hc = heads // chunks
    half = hc // 2
    w = half // 2
    hn = heads // n
    g = math.gcd(w, hn)
    vm = pltpu.VMEM
    dma = pltpu.SemaphoreType.DMA
    anyspace = pl.BlockSpec(memory_space=pl.ANY)
    vspec = pl.BlockSpec(memory_space=pltpu.VMEM)
    part = vm((chunks, w, D, D), BF16)
    fac = vm((2, 2, chunks * w, D), F32)
    scratch = [
        vm((tok, width), F32), vm((tok, width), F32),
        vm((2, tok, width), BF16), vm((2, tok, width), BF16),
        vm((heads, D, tok), BF16), vm((max(heads, D), tok), BF16), vm((1, width), F32),
        pltpu.SMEM(doc_lengths.shape, jnp.int32),
        vm((tok, tok), F32), vm((heads, tok), F32), vm((heads, tok), F32), vm((tok, D), F32), vm((tok, D), F32),
        fac, fac, fac, vm((chunks * w, D), F32),
        vm((hc // 2 * (chunks // LOADS), tok, tok), BF16),
        vm((chunks, 2, 2, w, D, D), BF16), vm((chunks, 2, w, D, D), BF16), vm((chunks, w, D, D), F32),
        part, part, part, part, part,
        vm((chunks, 2, w, D, D), BF16), vm((chunks, 2, w, D, D), BF16),
        vm((chunks, 2, 2, w, D, D), BF16),
        dma((LOADS,)), dma((LOADS,)), dma((3,)), dma((2,)), dma((2,)),
        dma, dma((chunks,)), dma, dma((chunks,)), dma, dma((chunks,)), dma, dma((chunks,)), dma, dma((chunks,)),
        dma, dma((hn // g,)), dma,
    ]
    mixed, squares, final = pl.pallas_call(
        functools.partial(kernel, n, heads, chunks),
        out_shape=(
            pltpu.VMEM((tok, width), BF16),
            pltpu.VMEM((tok, D), F32),
            pltpu.VMEM((hn, D, D), BF16),
        ),
        in_specs=[anyspace] * 7,
        out_specs=(vspec, vspec, vspec),
        scratch_shapes=scratch,
        compiler_params=pltpu.CompilerParams(
            collective_id=0, has_side_effects=True, vmem_limit_bytes=54 * 1024 * 1024
        ),
    )(queries, keys_in, values_in, gate_logits, log_decay.T, norm_gain.reshape(1, width), doc_lengths)
    rows = tok // FINISH_PARTS
    return pl.pallas_call(
        finish_kernel,
        out_shape=(
            jax.ShapeDtypeStruct((tok, width), BF16),
            jax.ShapeDtypeStruct((hn, D, D), F32),
        ),
        in_specs=[vspec, vspec, vspec],
        out_specs=(anyspace, anyspace),
        scratch_shapes=[
            vm((FINISH_PARTS, rows, width), BF16), vm((hn, D, D), F32), dma((FINISH_PARTS,)), dma,
        ],
        compiler_params=pltpu.CompilerParams(vmem_limit_bytes=16 * 1024 * 1024),
    )(mixed, squares, final)


def solution(mesh):
    rows = P(("grp", "seq"), None)
    return jax.shard_map(
        functools.partial(shards, mesh.shape["seq"]),
        mesh=mesh,
        in_specs=(rows, rows, rows, rows, rows, P(), P("grp")),
        out_specs=(rows, P(("grp", "seq"), None, None)),
        check_vma=False,
    )
```

```python
import functools
import math

import jax
import jax.numpy as jnp
from jax import lax
from jax.experimental import pallas as pl
from jax.experimental.pallas import tpu as pltpu
from jax.sharding import PartitionSpec as P

EPS = 1e-05
LOG2E = 1.4426950408889634
D = 128
GROUP = 4
CHUNKS = 16
LOADS = 8
CHAIN_LAG = 9
HOP_LAG = 4
E_LAG = 5
X_LAG = 1
SPREAD_EARLY = 2
FINISH_PARTS = 8
F32, BF16 = jnp.float32, jnp.bfloat16
MESH = pl.DeviceIdType.MESH


def dot(a, b, dims):
    return lax.dot_general(a, b, (dims, ((), ())), preferred_element_type=F32)


def diagonal(a, b):
    zero = jnp.zeros_like(a)
    return jnp.concatenate([jnp.concatenate([a, zero], axis=1), jnp.concatenate([zero, b], axis=1)], axis=0)


def kernel(
    n, heads, chunks,
    q_hbm, k_hbm, v_hbm, g_hbm, ld_hbm, gain_hbm, docs_hbm,
    out_s, ssq_s, fin_s,
    mix_s, gate_s, kv_s, qg_s, kt_s, ld_s, gain_s, docs_s, pen_s, cumt_s, kwt_s, cum_s, lead_s,
    fac_own, fac_core, fac_chip, fac_pair, wt_s, u_own, u_core, u_mine, u_send, u_pair, s_in, s_out, e_send, e_half,
    x_send, ent,
    load_sem, small_sem, fac_ss, fac_rs, core_ss, core_rs, pair_ss, pair_rs, z_ss, z_rs, e_ss, e_rs,
    x_ss, x_rs, f_ss, f_rs, f_ls,
):
    tok = q_hbm.shape[0]
    hc = heads // chunks
    half = hc // 2
    w = half // 2
    planes = n // GROUP
    loads = LOADS
    per = chunks // loads
    hn = heads // n
    g = math.gcd(w, hn)
    span = 2 * hn
    m = span // half
    me = lax.axis_index("seq")
    plane = me // GROUP
    r = me % GROUP
    y = r // 2
    c = r % 2
    core_peer = plane * GROUP + y * 2 + (1 - c)
    pair_peer = plane * GROUP + (1 - y) * 2 + c

    def send(src, dst, ss, rs, dev):
        return pltpu.make_async_remote_copy(
            src_ref=src, dst_ref=dst, send_sem=ss, recv_sem=rs,
            device_id={"seq": dev}, device_id_type=MESH,
        )

    def head0(j, yh):
        return (j // m) * (2 * span) + yh * span + (j % m) * half

    def hcol(j, yh, hh):
        return pl.ds(pl.multiple_of((head0(j, yh) + hh) * D, D), D)

    k_s, v_s = kv_s.at[0], kv_s.at[1]
    q_s, g_s = qg_s.at[0], qg_s.at[1]

    def fetch(first, second, both):
        def go(p, carry):
            for yh in range(2):
                at = pl.ds(pl.multiple_of(head0(p * per, yh) * D, half * per * D), half * per * D)
                pltpu.make_async_copy(first.at[:, at], both.at[0, :, at], load_sem.at[p]).start()
                pltpu.make_async_copy(second.at[:, at], both.at[1, :, at], load_sem.at[p]).start()
            return carry
        return go

    def fetched(both, sem, p):
        part = both.at[:, :, pl.ds(0, 2 * half * per * D)]
        pltpu.make_async_copy(part, part, sem.at[p]).wait()

    barrier = pltpu.get_barrier_semaphore()
    for d in range(1, GROUP):
        pl.semaphore_signal(
            barrier, inc=1, device_id={"seq": plane * GROUP + (r + d) % GROUP}, device_id_type=MESH
        )

    @pl.when(plane > 0)
    def _():
        pl.semaphore_signal(barrier, inc=1, device_id={"seq": me - GROUP}, device_id_type=MESH)

    ld_copy = pltpu.make_async_copy(ld_hbm, ld_s.at[pl.ds(0, heads)], small_sem.at[0])
    docs_copy = pltpu.make_async_copy(docs_hbm, docs_s, small_sem.at[1])
    gain_copy = pltpu.make_async_copy(gain_hbm, gain_s, small_sem.at[2])
    ld_copy.start()
    docs_copy.start()
    lax.fori_loop(0, loads, fetch(k_hbm, v_hbm, kv_s), 0)

    gain_copy.start()

    if heads < D:
        ld_s[pl.ds(heads, D - heads)] = jnp.zeros((D - heads, tok), BF16)
    base = me * tok
    row_i = lax.broadcasted_iota(jnp.int32, (tok, tok), 0)
    col_i = lax.broadcasted_iota(jnp.int32, (tok, tok), 1)
    causal = row_i >= col_i
    lanes = lax.broadcasted_iota(jnp.int32, (1, tok), 1)
    docs_copy.wait()
    n_docs = docs_s.shape[0]
    doc_row = jnp.zeros((1, tok), jnp.int32)
    before = jnp.int32(0)
    last = jnp.int32(0)
    end = jnp.int32(0)
    for d in range(n_docs):
        end = end + docs_s[d]
        doc_row = doc_row + jnp.where(lanes + base >= end, 1, 0)
        before = before + jnp.where(base - 1 >= end, 1, 0)
        last = last + jnp.where(base + tok - 1 >= end, 1, 0)
    closing = jnp.where(doc_row == last, 1.0, 0.0).astype(F32)
    ld_copy.wait()
    upper = jnp.where(row_i <= col_i, 1.0, 0.0).astype(BF16)
    cumt = dot(ld_s[pl.ds(0, heads)], upper, ((1,), (0,)))
    cumt_s[...] = LOG2E * cumt
    total = cumt[:, tok - 1:tok]
    kwt_s[...] = closing * jnp.exp(total - cumt)

    def updates(u):
        fetched(kv_s, load_sem, u)
        fetch(q_hbm, g_hbm, qg_s)(u, 0)

    def update_math(j):
        for yh in range(2):
            for hh in range(half):
                h = head0(j, yh) + hh
                kt = k_s[:, hcol(j, yh, hh)].T
                kt_s[h] = kt
                wk = (kt.astype(F32) * kwt_s[pl.ds(h, 1), :]).astype(BF16)
                up = dot(wk, v_s[:, hcol(j, yh, hh)], ((1,), (0,)))
                u_own[j, hh // w, yh, hh % w] = up.astype(BF16)

    def core_copy(j):
        return send(u_own.at[j, 1 - c], u_core.at[j], core_ss, core_rs.at[j], core_peer)

    def pair_copy(j):
        return send(u_send.at[j], u_pair.at[j], pair_ss, pair_rs.at[j], pair_peer)

    def z_copy(j):
        return send(s_out.at[j], s_in.at[j], z_ss, z_rs.at[j], (me + GROUP) % n)

    def e_copy(j):
        return send(e_send.at[j], e_half.at[j, y], e_ss, e_rs.at[j], pair_peer)

    def x_copy(j):
        at = pl.ds(j * per, per)
        return send(x_send.at[at], ent.at[at, c], x_ss, x_rs.at[j], core_peer)

    def fac_core_copy():
        return send(fac_own, fac_core, fac_ss.at[0], fac_rs.at[0], core_peer)

    def fac_pair_copy():
        return send(fac_chip.at[c, 1 - y], fac_pair, fac_ss.at[1], fac_rs.at[1], pair_peer)

    def combine(j):
        core_copy(j).wait_recv()
        for k in range(w):
            for yo in range(2):
                at = pl.ds(j * w + k, 1)
                fa = jnp.where(c == 0, fac_core[c, yo, at, :], 1.0)
                fb = jnp.where(c == 0, 1.0, fac_own[c, yo, at, :])
                val = fa * u_own[j, c, yo, k].astype(F32) + fb * u_core[j, yo, k].astype(F32)

                @pl.when(yo == y)
                def _():
                    u_mine[j, k] = val

                @pl.when(yo != y)
                def _():
                    u_send[j, k] = val.astype(BF16)
        pair_copy(j).start()

    def fin_place(j, s):
        h = head0(j, y) + c * w + s * g
        return h // hn, h % hn

    def fin_copy(j, s):
        dev, off = fin_place(j, s)
        return send(
            s_out.at[j, pl.ds(s * g, g)], fin_s.at[pl.ds(off, g)],
            f_ss, f_rs.at[off // g], dev,
        )

    def fin_local(j, s):
        _, off = fin_place(j, s)
        return pltpu.make_async_copy(s_out.at[j, pl.ds(s * g, g)], fin_s.at[pl.ds(off, g)], f_ls)

    def chain(j):
        @pl.when(j == 0)
        def _():
            fac_pair_copy().wait_recv()

        pair_copy(j).wait_recv()

        @pl.when(plane > 0)
        def _():
            z_copy(j).wait_recv()

        for k in range(w):
            at = pl.ds(j * w + k, 1)
            chip = fac_chip[c, y, at, :]
            other_chip = fac_pair[at, :]
            f01 = jnp.where(y == 0, chip, other_chip)
            f23 = jnp.where(y == 0, other_chip, chip)
            mine = u_mine[j, k]
            other = u_pair[j, k].astype(F32)
            entry = s_in[j, k].astype(F32)
            mid = f01 * entry + jnp.where(y == 0, mine, other)
            s_out[j, k] = (f23 * mid + jnp.where(y == 0, other, mine)).astype(BF16)
            e_send[j, k] = jnp.where(y == 0, mid, entry).astype(BF16)
            e_half[j, y, k] = jnp.where(y == 0, entry, mid).astype(BF16)

        @pl.when(plane < planes - 1)
        def _():
            z_copy(j).start()

        @pl.when(plane == planes - 1)
        def _():
            for s in range(w // g):
                dev, _off = fin_place(j, s)

                @pl.when(dev != me)
                def _():
                    fin_copy(j, s).start()

                @pl.when(dev == me)
                def _():
                    fin_local(j, s).start()
                    fin_local(j, s).wait()

    def inside_wait(i):
        @pl.when((i % 2 == 0) & (i < 2 * loads))
        def _():
            fetched(qg_s, load_sem, i // 2)

    def place(i):
        j = (i // 2) * per
        return j, i % 2, head0(j, i % 2)

    def wide(j, yh, hh):
        return pl.ds(pl.multiple_of((head0(j, yh) + hh) * D, 2 * D), 2 * D)

    def weigh(i):
        j, yh, h0 = place(i)
        blk = tok // 2
        cols = pltpu.roll(cum_s[...], (D - h0) % D, 1)
        for hh in range(0, half * per, 2):
            top = dot(
                q_s[:blk, wide(j, yh, hh)],
                diagonal(kt_s[h0 + hh, :, :blk], kt_s[h0 + hh + 1, :, :blk]), ((1,), (0,)),
            )
            for b in range(2):
                h = hh + b
                row = cumt_s[pl.ds(h0 + h, 1), :]
                ci = cols[:, h:h + 1]
                bot = dot(q_s[blk:, hcol(j, yh, h)], kt_s[h0 + h], ((1,), (0,)))
                at = slice(b * blk, (b + 1) * blk)
                wt_s[hh // 2, 0, :, at] = (
                    top[:, at] * jnp.exp2((ci[:blk] - row[:, :blk]) + pen_s[:blk, :blk])
                ).astype(BF16)
                wt_s[hh // 2, 1 + b] = (bot * jnp.exp2((ci[blk:] - row) + pen_s[blk:, :])).astype(BF16)

    def apply(i):
        j, yh, h0 = place(i)
        blk = tok // 2
        for hh in range(0, half * per, 2):
            both = wide(j, yh, hh)
            mix_s[:blk, both] = dot(
                wt_s[hh // 2, 0],
                diagonal(v_s[:blk, hcol(j, yh, hh)], v_s[:blk, hcol(j, yh, hh + 1)]), ((1,), (0,)),
            )
            for b in range(2):
                at = hcol(j, yh, hh + b)
                mix_s[blk:, at] = dot(wt_s[hh // 2, 1 + b], v_s[:, at], ((1,), (0,)))
            hg = 0.5 * gain_s[:, both]
            gate_s[:, both] = hg * jnp.tanh(0.5 * g_s[:, both].astype(F32)) + hg

    def share(j):
        @pl.when((plane > 0) | (y == 0))
        def _():
            e_copy(j).start()

    def spread(j):
        @pl.when((plane > 0) | (y == 1))
        def _():
            e_copy(j).wait_recv()

        for yo in range(2):
            for k in range(w):
                at = pl.ds(j * w + k, 1)
                f0 = jnp.where(c == 0, fac_own[c, yo, at, :], fac_core[c, yo, at, :])
                first = e_half[j, yo, k]
                u0 = jnp.where(c == 0, u_own[j, 0, yo, k], u_core[j, yo, k]).astype(F32)
                second = (f0 * first.astype(F32) + u0).astype(BF16)
                ent[j, c, yo, k] = jnp.where(c == 0, first, second)
                x_send[j, yo, k] = jnp.where(c == 0, second, first)

        @pl.when(j % per == per - 1)
        def _():
            x_copy(j // per).start()

    def across_wait(a):
        x_copy(a).wait_recv()

    def across(a):
        j = a * per
        cols = pltpu.roll(lead_s[...], (D - head0(j, 0)) % D, 1)
        acc = ssq_s[...]
        for yh in range(2):
            for hh in range(0, half * per, 2):
                entry = [ent[j + h // half, (h % half) // w, yh, h % w] for h in (hh, hh + 1)]
                both = dot(q_s[:, wide(j, yh, hh)], diagonal(*entry), ((1,), (0,)))
                for b in range(2):
                    at = hcol(j, yh, hh + b)
                    lane = yh * span + hh + b
                    mixed = mix_s[:, at] + cols[:, lane:lane + 1] * both[:, b * D:(b + 1) * D]
                    acc = acc + mixed * mixed
                    out_s[:, at] = (mixed * gate_s[:, at]).astype(BF16)
        ssq_s[...] = acc

    updates(0)
    update_math(0)
    own_f = jnp.where(last == before, 1.0, 0.0).astype(F32) * jnp.exp(jnp.broadcast_to(total, (heads, D)))
    for j in range(chunks):
        for yh in range(2):
            for cc in range(2):
                h = head0(j, yh) + cc * w
                fac_own[cc, yh, j * w:(j + 1) * w, :] = own_f[h:h + w]

    @pl.when(plane < planes - 1)
    def _():
        pl.semaphore_wait(barrier, GROUP)

    @pl.when(plane == planes - 1)
    def _():
        pl.semaphore_wait(barrier, GROUP - 1)

    core_copy(0).start()
    fac_core_copy().start()
    for j in range(1, per):
        update_math(j)
        core_copy(j).start()
    updates(1)
    for j in range(per, 2 * per):
        update_math(j)
        core_copy(j).start()
    fac_core_copy().wait_recv()
    fac_chip[...] = fac_own[...] * fac_core[...]
    fac_pair_copy().start()
    for j in range(per):
        combine(j)

    rows = lax.broadcasted_iota(jnp.int32, (tok, D), 0)
    doc_col = jnp.zeros((tok, D), jnp.int32)
    end = jnp.int32(0)
    for d in range(n_docs):
        end = end + docs_s[d]
        doc_col = doc_col + jnp.where(rows + base >= end, 1, 0)
    pen_s[...] = jnp.where(causal & (doc_col[:, :1] == doc_row), 0.0, -1e30).astype(F32)
    tri = jnp.where(causal, 1.0, 0.0).astype(BF16)
    cum = dot(tri, ld_s[...], ((1,), (1,)))
    cum_s[...] = LOG2E * cum
    lead_s[...] = jnp.where(doc_col == before, 1.0, 0.0).astype(F32) * jnp.exp(cum)
    ssq_s[...] = jnp.zeros_like(ssq_s)

    @pl.when(plane == 0)
    def _():
        s_in[...] = jnp.zeros_like(s_in)

    @pl.when((plane == 0) & (y == 0))
    def _():
        e_half[:, 1] = jnp.zeros(e_half.shape[:1] + e_half.shape[2:], BF16)

    gain_copy.wait()
    for j in range(per, 2 * per):
        combine(j)
    updates(2)
    inside_wait(0)
    for j in range(2 * per, 3 * per):
        update_math(j)
    weigh(0)
    for j in range(2 * per, 3 * per):
        core_copy(j).start()

    chain_lag = 9 + 4 * plane + 2 * (plane // (planes - 1))
    e_lag = jnp.maximum(chain_lag, chunks + per + 1)
    ends = jnp.where(plane == planes - 1, 0, chain_lag + chunks - SPREAD_EARLY)
    spread_lag = jnp.maximum(e_lag + E_LAG, ends)
    across_lag = (spread_lag + X_LAG + 2) // 2 * 2 + 1
    steps = jnp.maximum(across_lag + chunks, (2 * loads + 3) * per)

    def step(t, carry):
        def at(lag, count, body, first=0):
            @pl.when((t >= lag + first) & (t < lag + count))
            def _():
                body(t - lag)

        at(per + 1, chunks, combine, 2 * per)
        at(chain_lag, chunks, chain)
        at(e_lag, chunks, share)
        at(spread_lag, chunks, spread)

        u = t // per
        a = (t - across_lag) // per
        even = t % per == 0
        odd = t % per == 1
        states = odd & (t >= across_lag) & (t < across_lag + chunks)

        @pl.when(even & (u < loads))
        def _():
            updates(u)
            inside_wait(u - 2)
            for j in range(per):
                update_math(t + j)
            apply(u - 3)
            weigh(u - 2)
            for j in range(per):
                core_copy(t + j).start()

        i = t - chunks + loads - 2

        @pl.when((t >= chunks) & (i < 2 * loads))
        def _():
            inside_wait(i)
            apply(i - 1)
            weigh(i)

        @pl.when(i == 2 * loads)
        def _():
            apply(i - 1)

        @pl.when(states)
        def _():
            across_wait(a)
            across(a)

        return carry

    lax.fori_loop(3 * per, steps, step, 0)

    mean = jnp.sum(ssq_s[...], axis=1, keepdims=True) * (1.0 / (heads * D))
    ssq_s[...] = jnp.broadcast_to(lax.rsqrt(mean + EPS), (tok, D))

    for s in range(hn // g):
        h = me * hn + s * g
        src = (planes - 1) * GROUP + ((h // span) % 2) * 2 + (h % half) // w

        @pl.when(src != me)
        def _():
            send(
                s_out.at[0, pl.ds(0, g)], fin_s.at[pl.ds(s * g, g)], f_ss, f_rs.at[s], core_peer
            ).wait_recv()

    fac_core_copy().wait_send()
    fac_pair_copy().wait_send()
    send(u_own.at[:, 1 - c], u_core, core_ss, core_rs.at[0], core_peer).wait_send()
    send(u_send, u_pair, pair_ss, pair_rs.at[0], pair_peer).wait_send()

    @pl.when((plane > 0) | (y == 0))
    def _():
        send(e_send, s_in, e_ss, e_rs.at[0], pair_peer).wait_send()

    send(x_send, e_half, x_ss, x_rs.at[0], core_peer).wait_send()

    @pl.when(plane < planes - 1)
    def _():
        send(s_out, s_in, z_ss, z_rs.at[0], (me + GROUP) % n).wait_send()

    @pl.when(plane == planes - 1)
    def _():
        sent = pl.ds(0, chunks - max(1, hn // (2 * w)))
        send(s_out.at[sent], s_in.at[sent], f_ss, f_rs.at[0], core_peer).wait_send()


def finish_kernel(mix_ref, inv_ref, fin_in, out_hbm, fin_hbm, buf, fin_s, sem, fin_sem):
    parts = buf.shape[0]
    rows = buf.shape[1]
    fin_s[...] = fin_in[...].astype(F32)
    fin_copy = pltpu.make_async_copy(fin_s, fin_hbm, fin_sem)
    fin_copy.start()
    copies = [fin_copy]
    for p in range(parts):
        at = slice(p * rows, (p + 1) * rows)
        inv = inv_ref[at, :]
        for t in range(mix_ref.shape[1] // D):
            cols = slice(t * D, (t + 1) * D)
            buf[p, :, cols] = (mix_ref[at, cols].astype(F32) * inv).astype(BF16)
        copy = pltpu.make_async_copy(buf.at[p], out_hbm.at[pl.ds(p * rows, rows)], sem.at[p])
        copy.start()
        copies.append(copy)
    for copy in copies:
        copy.wait()


def shards(n, queries, keys_in, values_in, log_decay, gate_logits, norm_gain, doc_lengths):
    tok, width = queries.shape
    heads = width // D
    chunks = CHUNKS
    hc = heads // chunks
    half = hc // 2
    w = half // 2
    hn = heads // n
    g = math.gcd(w, hn)
    vm = pltpu.VMEM
    dma = pltpu.SemaphoreType.DMA
    anyspace = pl.BlockSpec(memory_space=pl.ANY)
    vspec = pl.BlockSpec(memory_space=pltpu.VMEM)
    part = vm((chunks, w, D, D), BF16)
    fac = vm((2, 2, chunks * w, D), F32)
    scratch = [
        vm((tok, width), F32), vm((tok, width), F32),
        vm((2, tok, width), BF16), vm((2, tok, width), BF16),
        vm((heads, D, tok), BF16), vm((max(heads, D), tok), BF16), vm((1, width), F32),
        pltpu.SMEM(doc_lengths.shape, jnp.int32),
        vm((tok, tok), F32), vm((heads, tok), F32), vm((heads, tok), F32), vm((tok, D), F32), vm((tok, D), F32),
        fac, fac, fac, vm((chunks * w, D), F32),
        vm((hc // 4 * (chunks // LOADS), 3, tok // 2, tok), BF16),
        vm((chunks, 2, 2, w, D, D), BF16), vm((chunks, 2, w, D, D), BF16), vm((chunks, w, D, D), F32),
        part, part, part, part, part,
        vm((chunks, 2, w, D, D), BF16), vm((chunks, 2, w, D, D), BF16),
        vm((chunks, 2, 2, w, D, D), BF16),
        dma((LOADS,)), dma((3,)), dma((2,)), dma((2,)),
        dma, dma((chunks,)), dma, dma((chunks,)), dma, dma((chunks,)), dma, dma((chunks,)), dma, dma((LOADS,)),
        dma, dma((hn // g,)), dma,
    ]
    mixed, squares, final = pl.pallas_call(
        functools.partial(kernel, n, heads, chunks),
        out_shape=(
            pltpu.VMEM((tok, width), BF16),
            pltpu.VMEM((tok, D), F32),
            pltpu.VMEM((hn, D, D), BF16),
        ),
        in_specs=[anyspace] * 7,
        out_specs=(vspec, vspec, vspec),
        scratch_shapes=scratch,
        compiler_params=pltpu.CompilerParams(
            collective_id=0, has_side_effects=True, vmem_limit_bytes=54 * 1024 * 1024
        ),
    )(queries, keys_in, values_in, gate_logits, log_decay.T, norm_gain.reshape(1, width), doc_lengths)
    rows = tok // FINISH_PARTS
    return pl.pallas_call(
        finish_kernel,
        out_shape=(
            jax.ShapeDtypeStruct((tok, width), BF16),
            jax.ShapeDtypeStruct((hn, D, D), F32),
        ),
        in_specs=[vspec, vspec, vspec],
        out_specs=(anyspace, anyspace),
        scratch_shapes=[
            vm((FINISH_PARTS, rows, width), BF16), vm((hn, D, D), F32), dma((FINISH_PARTS,)), dma,
        ],
        compiler_params=pltpu.CompilerParams(vmem_limit_bytes=16 * 1024 * 1024),
    )(mixed, squares, final)


def solution(mesh):
    rows = P(("grp", "seq"), None)
    return jax.shard_map(
        functools.partial(shards, mesh.shape["seq"]),
        mesh=mesh,
        in_specs=(rows, rows, rows, rows, rows, P(), P("grp")),
        out_specs=(rows, P(("grp", "seq"), None, None)),
        check_vma=False,
    )
```

```python
import functools
import math

import jax
import jax.numpy as jnp
from jax import lax
from jax.experimental import pallas as pl
from jax.experimental.pallas import tpu as pltpu
from jax.sharding import PartitionSpec as P

EPS = 1e-05
LOG2E = 1.4426950408889634
D = 128
GROUP = 4
CHUNKS = 16
LOADS = 8
CHAIN_LAG = 9
HOP_LAG = 4
E_LAG = 5
X_LAG = 1
SPREAD_EARLY = 8
FINISH_PARTS = 8
F32, BF16 = jnp.float32, jnp.bfloat16
MESH = pl.DeviceIdType.MESH


def dot(a, b, dims):
    return lax.dot_general(a, b, (dims, ((), ())), preferred_element_type=F32)


def diagonal(a, b):
    zero = jnp.zeros_like(a)
    return jnp.concatenate([jnp.concatenate([a, zero], axis=1), jnp.concatenate([zero, b], axis=1)], axis=0)


def kernel(
    n, heads, chunks,
    q_hbm, k_hbm, v_hbm, g_hbm, ld_hbm, gain_hbm, docs_hbm,
    out_s, ssq_s, fin_s,
    mix_s, gate_s, kv_s, qg_s, kt_s, ld_s, gain_s, docs_s, pen_s, cumt_s, kwt_s, cum_s, lead_s,
    fac_own, fac_core, fac_chip, fac_pair, wt_s, u_own, u_core, u_mine, u_send, u_pair, s_in, s_out, e_send, e_half,
    x_send, ent,
    load_sem, small_sem, fac_ss, fac_rs, core_ss, core_rs, pair_ss, pair_rs, z_ss, z_rs, e_ss, e_rs,
    x_ss, x_rs, f_ss, f_rs, f_ls,
):
    tok = q_hbm.shape[0]
    hc = heads // chunks
    half = hc // 2
    w = half // 2
    planes = n // GROUP
    loads = LOADS
    per = chunks // loads
    hn = heads // n
    g = math.gcd(w, hn)
    span = 2 * hn
    m = span // half
    me = lax.axis_index("seq")
    plane = me // GROUP
    r = me % GROUP
    y = r // 2
    c = r % 2
    core_peer = plane * GROUP + y * 2 + (1 - c)
    pair_peer = plane * GROUP + (1 - y) * 2 + c

    def send(src, dst, ss, rs, dev):
        return pltpu.make_async_remote_copy(
            src_ref=src, dst_ref=dst, send_sem=ss, recv_sem=rs,
            device_id={"seq": dev}, device_id_type=MESH,
        )

    def head0(j, yh):
        return (j // m) * (2 * span) + yh * span + (j % m) * half

    def hcol(j, yh, hh):
        return pl.ds(pl.multiple_of((head0(j, yh) + hh) * D, D), D)

    k_s, v_s = kv_s.at[0], kv_s.at[1]
    q_s, g_s = qg_s.at[0], qg_s.at[1]

    def fetch(first, second, both):
        def go(p, carry):
            for yh in range(2):
                at = pl.ds(pl.multiple_of(head0(p * per, yh) * D, half * per * D), half * per * D)
                pltpu.make_async_copy(first.at[:, at], both.at[0, :, at], load_sem.at[p]).start()
                pltpu.make_async_copy(second.at[:, at], both.at[1, :, at], load_sem.at[p]).start()
            return carry
        return go

    def fetched(both, sem, p):
        part = both.at[:, :, pl.ds(0, 2 * half * per * D)]
        pltpu.make_async_copy(part, part, sem.at[p]).wait()

    barrier = pltpu.get_barrier_semaphore()
    for d in range(1, GROUP):
        pl.semaphore_signal(
            barrier, inc=1, device_id={"seq": plane * GROUP + (r + d) % GROUP}, device_id_type=MESH
        )

    @pl.when(plane > 0)
    def _():
        pl.semaphore_signal(barrier, inc=1, device_id={"seq": me - GROUP}, device_id_type=MESH)

    ld_copy = pltpu.make_async_copy(ld_hbm, ld_s.at[pl.ds(0, heads)], small_sem.at[0])
    docs_copy = pltpu.make_async_copy(docs_hbm, docs_s, small_sem.at[1])
    gain_copy = pltpu.make_async_copy(gain_hbm, gain_s, small_sem.at[2])
    ld_copy.start()
    docs_copy.start()
    lax.fori_loop(0, loads, fetch(k_hbm, v_hbm, kv_s), 0)

    gain_copy.start()

    if heads < D:
        ld_s[pl.ds(heads, D - heads)] = jnp.zeros((D - heads, tok), BF16)
    base = me * tok
    row_i = lax.broadcasted_iota(jnp.int32, (tok, tok), 0)
    col_i = lax.broadcasted_iota(jnp.int32, (tok, tok), 1)
    causal = row_i >= col_i
    lanes = lax.broadcasted_iota(jnp.int32, (1, tok), 1)
    docs_copy.wait()
    n_docs = docs_s.shape[0]
    doc_row = jnp.zeros((1, tok), jnp.int32)
    before = jnp.int32(0)
    last = jnp.int32(0)
    end = jnp.int32(0)
    for d in range(n_docs):
        end = end + docs_s[d]
        doc_row = doc_row + jnp.where(lanes + base >= end, 1, 0)
        before = before + jnp.where(base - 1 >= end, 1, 0)
        last = last + jnp.where(base + tok - 1 >= end, 1, 0)
    closing = jnp.where(doc_row == last, 1.0, 0.0).astype(F32)
    ld_copy.wait()
    upper = jnp.where(row_i <= col_i, 1.0, 0.0).astype(BF16)
    cumt = dot(ld_s[pl.ds(0, heads)], upper, ((1,), (0,)))
    cumt_s[...] = LOG2E * cumt
    total = cumt[:, tok - 1:tok]
    kwt_s[...] = closing * jnp.exp(total - cumt)

    def updates(u):
        fetched(kv_s, load_sem, u)
        fetch(q_hbm, g_hbm, qg_s)(u, 0)

    def update_math(j):
        for yh in range(2):
            for hh in range(half):
                h = head0(j, yh) + hh
                kt = k_s[:, hcol(j, yh, hh)].T
                kt_s[h] = kt
                wk = (kt.astype(F32) * kwt_s[pl.ds(h, 1), :]).astype(BF16)
                up = dot(wk, v_s[:, hcol(j, yh, hh)], ((1,), (0,)))
                u_own[j, hh // w, yh, hh % w] = up.astype(BF16)

    def core_copy(j):
        return send(u_own.at[j, 1 - c], u_core.at[j], core_ss, core_rs.at[j], core_peer)

    def pair_copy(j):
        return send(u_send.at[j], u_pair.at[j], pair_ss, pair_rs.at[j], pair_peer)

    def z_copy(j):
        return send(s_out.at[j], s_in.at[j], z_ss, z_rs.at[j], (me + GROUP) % n)

    def e_copy(j):
        return send(e_send.at[j], e_half.at[j, y], e_ss, e_rs.at[j], pair_peer)

    def x_copy(j):
        at = pl.ds(j * per, per)
        return send(x_send.at[at], ent.at[at, c], x_ss, x_rs.at[j], core_peer)

    def fac_core_copy():
        return send(fac_own, fac_core, fac_ss.at[0], fac_rs.at[0], core_peer)

    def fac_pair_copy():
        return send(fac_chip.at[c, 1 - y], fac_pair, fac_ss.at[1], fac_rs.at[1], pair_peer)

    def combine(j):
        core_copy(j).wait_recv()
        for k in range(w):
            for yo in range(2):
                at = pl.ds(j * w + k, 1)
                fa = jnp.where(c == 0, fac_core[c, yo, at, :], 1.0)
                fb = jnp.where(c == 0, 1.0, fac_own[c, yo, at, :])
                val = fa * u_own[j, c, yo, k].astype(F32) + fb * u_core[j, yo, k].astype(F32)

                @pl.when(yo == y)
                def _():
                    u_mine[j, k] = val

                @pl.when(yo != y)
                def _():
                    u_send[j, k] = val.astype(BF16)
        pair_copy(j).start()

    def fin_place(j, s):
        h = head0(j, y) + c * w + s * g
        return h // hn, h % hn

    def fin_copy(j, s):
        dev, off = fin_place(j, s)
        return send(
            s_out.at[j, pl.ds(s * g, g)], fin_s.at[pl.ds(off, g)],
            f_ss, f_rs.at[off // g], dev,
        )

    def fin_local(j, s):
        _, off = fin_place(j, s)
        return pltpu.make_async_copy(s_out.at[j, pl.ds(s * g, g)], fin_s.at[pl.ds(off, g)], f_ls)

    def chain(j):
        @pl.when(j == 0)
        def _():
            fac_pair_copy().wait_recv()

        pair_copy(j).wait_recv()

        @pl.when(plane > 0)
        def _():
            z_copy(j).wait_recv()

        for k in range(w):
            at = pl.ds(j * w + k, 1)
            chip = fac_chip[c, y, at, :]
            other_chip = fac_pair[at, :]
            f01 = jnp.where(y == 0, chip, other_chip)
            f23 = jnp.where(y == 0, other_chip, chip)
            mine = u_mine[j, k]
            other = u_pair[j, k].astype(F32)
            entry = s_in[j, k].astype(F32)
            mid = f01 * entry + jnp.where(y == 0, mine, other)
            s_out[j, k] = (f23 * mid + jnp.where(y == 0, other, mine)).astype(BF16)
            e_send[j, k] = jnp.where(y == 0, mid, entry).astype(BF16)
            e_half[j, y, k] = jnp.where(y == 0, entry, mid).astype(BF16)

        @pl.when(plane < planes - 1)
        def _():
            z_copy(j).start()

        @pl.when(plane == planes - 1)
        def _():
            for s in range(w // g):
                dev, _off = fin_place(j, s)

                @pl.when(dev != me)
                def _():
                    fin_copy(j, s).start()

                @pl.when(dev == me)
                def _():
                    fin_local(j, s).start()
                    fin_local(j, s).wait()

    def inside_wait(i):
        @pl.when((i % 2 == 0) & (i < 2 * loads))
        def _():
            fetched(qg_s, load_sem, i // 2)

    def place(i):
        j = (i // 2) * per
        return j, i % 2, head0(j, i % 2)

    def wide(j, yh, hh):
        return pl.ds(pl.multiple_of((head0(j, yh) + hh) * D, 2 * D), 2 * D)

    def weigh(i):
        j, yh, h0 = place(i)
        blk = tok // 2
        cols = pltpu.roll(cum_s[...], (D - h0) % D, 1)
        for hh in range(0, half * per, 2):
            top = dot(
                q_s[:blk, wide(j, yh, hh)],
                diagonal(kt_s[h0 + hh, :, :blk], kt_s[h0 + hh + 1, :, :blk]), ((1,), (0,)),
            )
            for b in range(2):
                h = hh + b
                row = cumt_s[pl.ds(h0 + h, 1), :]
                ci = cols[:, h:h + 1]
                bot = dot(q_s[blk:, hcol(j, yh, h)], kt_s[h0 + h], ((1,), (0,)))
                at = slice(b * blk, (b + 1) * blk)
                wt_s[hh // 2, 0, :, at] = (
                    top[:, at] * jnp.exp2((ci[:blk] - row[:, :blk]) + pen_s[:blk, :blk])
                ).astype(BF16)
                wt_s[hh // 2, 1 + b] = (bot * jnp.exp2((ci[blk:] - row) + pen_s[blk:, :])).astype(BF16)

    def apply(i):
        j, yh, h0 = place(i)
        blk = tok // 2
        for hh in range(0, half * per, 2):
            both = wide(j, yh, hh)
            mix_s[:blk, both] = dot(
                wt_s[hh // 2, 0],
                diagonal(v_s[:blk, hcol(j, yh, hh)], v_s[:blk, hcol(j, yh, hh + 1)]), ((1,), (0,)),
            )
            for b in range(2):
                at = hcol(j, yh, hh + b)
                mix_s[blk:, at] = dot(wt_s[hh // 2, 1 + b], v_s[:, at], ((1,), (0,)))
            hg = 0.5 * gain_s[:, both]
            gate_s[:, both] = hg * jnp.tanh(0.5 * g_s[:, both].astype(F32)) + hg

    def share(j):
        @pl.when((plane > 0) | (y == 0))
        def _():
            e_copy(j).start()

    def spread(j):
        @pl.when((plane > 0) | (y == 1))
        def _():
            e_copy(j).wait_recv()

        for yo in range(2):
            for k in range(w):
                at = pl.ds(j * w + k, 1)
                f0 = jnp.where(c == 0, fac_own[c, yo, at, :], fac_core[c, yo, at, :])
                first = e_half[j, yo, k]
                u0 = jnp.where(c == 0, u_own[j, 0, yo, k], u_core[j, yo, k]).astype(F32)
                second = (f0 * first.astype(F32) + u0).astype(BF16)
                ent[j, c, yo, k] = jnp.where(c == 0, first, second)
                x_send[j, yo, k] = jnp.where(c == 0, second, first)

        @pl.when(j % per == per - 1)
        def _():
            x_copy(j // per).start()

    def across_wait(a):
        x_copy(a).wait_recv()

    def across(a):
        j = a * per
        cols = pltpu.roll(lead_s[...], (D - head0(j, 0)) % D, 1)
        acc = ssq_s[...]
        for yh in range(2):
            for hh in range(0, half * per, 2):
                entry = [ent[j + h // half, (h % half) // w, yh, h % w] for h in (hh, hh + 1)]
                both = dot(q_s[:, wide(j, yh, hh)], diagonal(*entry), ((1,), (0,)))
                for b in range(2):
                    at = hcol(j, yh, hh + b)
                    lane = yh * span + hh + b
                    mixed = mix_s[:, at] + cols[:, lane:lane + 1] * both[:, b * D:(b + 1) * D]
                    acc = acc + mixed * mixed
                    out_s[:, at] = (mixed * gate_s[:, at]).astype(BF16)
        ssq_s[...] = acc

    updates(0)
    update_math(0)
    own_f = jnp.where(last == before, 1.0, 0.0).astype(F32) * jnp.exp(jnp.broadcast_to(total, (heads, D)))
    for j in range(chunks):
        for yh in range(2):
            for cc in range(2):
                h = head0(j, yh) + cc * w
                fac_own[cc, yh, j * w:(j + 1) * w, :] = own_f[h:h + w]

    @pl.when(plane < planes - 1)
    def _():
        pl.semaphore_wait(barrier, GROUP)

    @pl.when(plane == planes - 1)
    def _():
        pl.semaphore_wait(barrier, GROUP - 1)

    core_copy(0).start()
    fac_core_copy().start()
    for j in range(1, per):
        update_math(j)
        core_copy(j).start()
    updates(1)
    for j in range(per, 2 * per):
        update_math(j)
        core_copy(j).start()
    fac_core_copy().wait_recv()
    fac_chip[...] = fac_own[...] * fac_core[...]
    fac_pair_copy().start()
    for j in range(per):
        combine(j)

    rows = lax.broadcasted_iota(jnp.int32, (tok, D), 0)
    doc_col = jnp.zeros((tok, D), jnp.int32)
    end = jnp.int32(0)
    for d in range(n_docs):
        end = end + docs_s[d]
        doc_col = doc_col + jnp.where(rows + base >= end, 1, 0)
    pen_s[...] = jnp.where(causal & (doc_col[:, :1] == doc_row), 0.0, -1e30).astype(F32)
    tri = jnp.where(causal, 1.0, 0.0).astype(BF16)
    cum = dot(tri, ld_s[...], ((1,), (1,)))
    cum_s[...] = LOG2E * cum
    lead_s[...] = jnp.where(doc_col == before, 1.0, 0.0).astype(F32) * jnp.exp(cum)
    ssq_s[...] = jnp.zeros_like(ssq_s)

    @pl.when(plane == 0)
    def _():
        s_in[...] = jnp.zeros_like(s_in)

    @pl.when((plane == 0) & (y == 0))
    def _():
        e_half[:, 1] = jnp.zeros(e_half.shape[:1] + e_half.shape[2:], BF16)

    gain_copy.wait()
    for j in range(per, 2 * per):
        combine(j)
    updates(2)
    inside_wait(0)
    for j in range(2 * per, 3 * per):
        update_math(j)
    weigh(0)
    for j in range(2 * per, 3 * per):
        core_copy(j).start()

    chain_lag = 9 + 4 * plane + 2 * (plane // (planes - 1))
    e_lag = jnp.maximum(chain_lag, chunks + per + 1)
    ends = jnp.where(plane == planes - 1, 0, chain_lag + chunks - SPREAD_EARLY)
    spread_lag = jnp.maximum(e_lag + E_LAG, ends)
    across_lag = (spread_lag + X_LAG + 2) // 2 * 2 + 1
    steps = jnp.maximum(across_lag + chunks, (2 * loads + 3) * per)

    def step(t, carry):
        def at(lag, count, body, first=0):
            @pl.when((t >= lag + first) & (t < lag + count))
            def _():
                body(t - lag)

        at(per + 1, chunks, combine, 2 * per)
        at(chain_lag, chunks, chain)
        at(e_lag, chunks, share)
        at(spread_lag, chunks, spread)

        u = t // per
        a = (t - across_lag) // per
        even = t % per == 0
        odd = t % per == 1
        states = odd & (t >= across_lag) & (t < across_lag + chunks)

        @pl.when(even & (u < loads))
        def _():
            updates(u)
            inside_wait(u - 2)
            for j in range(per):
                update_math(t + j)
            apply(u - 3)
            weigh(u - 2)
            for j in range(per):
                core_copy(t + j).start()

        i = t - chunks + loads - 2

        @pl.when((t >= chunks) & (i < 2 * loads))
        def _():
            inside_wait(i)
            apply(i - 1)
            weigh(i)

        @pl.when(i == 2 * loads)
        def _():
            apply(i - 1)

        @pl.when(states)
        def _():
            across_wait(a)
            across(a)

        return carry

    lax.fori_loop(3 * per, steps, step, 0)

    mean = jnp.sum(ssq_s[...], axis=1, keepdims=True) * (1.0 / (heads * D))
    ssq_s[...] = jnp.broadcast_to(lax.rsqrt(mean + EPS), (tok, D))

    for s in range(hn // g):
        h = me * hn + s * g
        src = (planes - 1) * GROUP + ((h // span) % 2) * 2 + (h % half) // w

        @pl.when(src != me)
        def _():
            send(
                s_out.at[0, pl.ds(0, g)], fin_s.at[pl.ds(s * g, g)], f_ss, f_rs.at[s], core_peer
            ).wait_recv()

    fac_core_copy().wait_send()
    fac_pair_copy().wait_send()
    send(u_own.at[:, 1 - c], u_core, core_ss, core_rs.at[0], core_peer).wait_send()
    send(u_send, u_pair, pair_ss, pair_rs.at[0], pair_peer).wait_send()

    @pl.when((plane > 0) | (y == 0))
    def _():
        send(e_send, s_in, e_ss, e_rs.at[0], pair_peer).wait_send()

    send(x_send, e_half, x_ss, x_rs.at[0], core_peer).wait_send()

    @pl.when(plane < planes - 1)
    def _():
        send(s_out, s_in, z_ss, z_rs.at[0], (me + GROUP) % n).wait_send()

    @pl.when(plane == planes - 1)
    def _():
        sent = pl.ds(0, chunks - max(1, hn // (2 * w)))
        send(s_out.at[sent], s_in.at[sent], f_ss, f_rs.at[0], core_peer).wait_send()


def finish_kernel(mix_ref, inv_ref, fin_in, out_hbm, fin_hbm, buf, fin_s, sem, fin_sem):
    parts = buf.shape[0]
    rows = buf.shape[1]
    fin_s[...] = fin_in[...].astype(F32)
    fin_copy = pltpu.make_async_copy(fin_s, fin_hbm, fin_sem)
    fin_copy.start()
    copies = [fin_copy]
    for p in range(parts):
        at = slice(p * rows, (p + 1) * rows)
        inv = inv_ref[at, :]
        for t in range(mix_ref.shape[1] // D):
            cols = slice(t * D, (t + 1) * D)
            buf[p, :, cols] = (mix_ref[at, cols].astype(F32) * inv).astype(BF16)
        copy = pltpu.make_async_copy(buf.at[p], out_hbm.at[pl.ds(p * rows, rows)], sem.at[p])
        copy.start()
        copies.append(copy)
    for copy in copies:
        copy.wait()


def shards(n, queries, keys_in, values_in, log_decay, gate_logits, norm_gain, doc_lengths):
    tok, width = queries.shape
    heads = width // D
    chunks = CHUNKS
    hc = heads // chunks
    half = hc // 2
    w = half // 2
    hn = heads // n
    g = math.gcd(w, hn)
    vm = pltpu.VMEM
    dma = pltpu.SemaphoreType.DMA
    anyspace = pl.BlockSpec(memory_space=pl.ANY)
    vspec = pl.BlockSpec(memory_space=pltpu.VMEM)
    part = vm((chunks, w, D, D), BF16)
    fac = vm((2, 2, chunks * w, D), F32)
    scratch = [
        vm((tok, width), F32), vm((tok, width), F32),
        vm((2, tok, width), BF16), vm((2, tok, width), BF16),
        vm((heads, D, tok), BF16), vm((max(heads, D), tok), BF16), vm((1, width), F32),
        pltpu.SMEM(doc_lengths.shape, jnp.int32),
        vm((tok, tok), F32), vm((heads, tok), F32), vm((heads, tok), F32), vm((tok, D), F32), vm((tok, D), F32),
        fac, fac, fac, vm((chunks * w, D), F32),
        vm((hc // 4 * (chunks // LOADS), 3, tok // 2, tok), BF16),
        vm((chunks, 2, 2, w, D, D), BF16), vm((chunks, 2, w, D, D), BF16), vm((chunks, w, D, D), F32),
        part, part, part, part, part,
        vm((chunks, 2, w, D, D), BF16), vm((chunks, 2, w, D, D), BF16),
        vm((chunks, 2, 2, w, D, D), BF16),
        dma((LOADS,)), dma((3,)), dma((2,)), dma((2,)),
        dma, dma((chunks,)), dma, dma((chunks,)), dma, dma((chunks,)), dma, dma((chunks,)), dma, dma((LOADS,)),
        dma, dma((hn // g,)), dma,
    ]
    mixed, squares, final = pl.pallas_call(
        functools.partial(kernel, n, heads, chunks),
        out_shape=(
            pltpu.VMEM((tok, width), BF16),
            pltpu.VMEM((tok, D), F32),
            pltpu.VMEM((hn, D, D), BF16),
        ),
        in_specs=[anyspace] * 7,
        out_specs=(vspec, vspec, vspec),
        scratch_shapes=scratch,
        compiler_params=pltpu.CompilerParams(
            collective_id=0, has_side_effects=True, vmem_limit_bytes=54 * 1024 * 1024
        ),
    )(queries, keys_in, values_in, gate_logits, log_decay.T, norm_gain.reshape(1, width), doc_lengths)
    rows = tok // FINISH_PARTS
    return pl.pallas_call(
        finish_kernel,
        out_shape=(
            jax.ShapeDtypeStruct((tok, width), BF16),
            jax.ShapeDtypeStruct((hn, D, D), F32),
        ),
        in_specs=[vspec, vspec, vspec],
        out_specs=(anyspace, anyspace),
        scratch_shapes=[
            vm((FINISH_PARTS, rows, width), BF16), vm((hn, D, D), F32), dma((FINISH_PARTS,)), dma,
        ],
        compiler_params=pltpu.CompilerParams(vmem_limit_bytes=16 * 1024 * 1024),
    )(mixed, squares, final)


def solution(mesh):
    rows = P(("grp", "seq"), None)
    return jax.shard_map(
        functools.partial(shards, mesh.shape["seq"]),
        mesh=mesh,
        in_specs=(rows, rows, rows, rows, rows, P(), P("grp")),
        out_specs=(rows, P(("grp", "seq"), None, None)),
        check_vma=False,
    )
```

```python
import functools
import math

import jax
import jax.numpy as jnp
from jax import lax
from jax.experimental import pallas as pl
from jax.experimental.pallas import tpu as pltpu
from jax.sharding import PartitionSpec as P

EPS = 1e-05
LOG2E = 1.4426950408889634
D = 128
GROUP = 4
CHUNKS = 16
LOADS = 8
AHEAD = 3
CHAIN_LAG = 9
HOP_LAG = 4
E_LAG = 5
X_LAG = 1
SPREAD_EARLY = 8
FINISH_PARTS = 8
F32, BF16 = jnp.float32, jnp.bfloat16
MESH = pl.DeviceIdType.MESH


def dot(a, b, dims):
    return lax.dot_general(a, b, (dims, ((), ())), preferred_element_type=F32)


def diagonal(a, b):
    zero = jnp.zeros_like(a)
    return jnp.concatenate([jnp.concatenate([a, zero], axis=1), jnp.concatenate([zero, b], axis=1)], axis=0)


def kernel(
    n, heads, chunks,
    q_hbm, k_hbm, v_hbm, g_hbm, ld_hbm, gain_hbm, docs_hbm,
    out_s, ssq_s, fin_s,
    mix_s, gate_s, kv_s, qg_s, kt_s, ld_s, gain_s, docs_s, pen_s, cumt_s, kwt_s, cum_s, lead_s,
    fac_own, fac_core, fac_chip, fac_pair, wt_s, u_own, u_core, u_mine, u_send, u_pair, s_in, s_out, e_send, e_half,
    x_send, ent,
    load_sem, small_sem, fac_ss, fac_rs, core_ss, core_rs, pair_ss, pair_rs, z_ss, z_rs, e_ss, e_rs,
    x_ss, x_rs, f_ss, f_rs, f_ls,
):
    tok = q_hbm.shape[0]
    hc = heads // chunks
    half = hc // 2
    w = half // 2
    planes = n // GROUP
    loads = LOADS
    per = chunks // loads
    hn = heads // n
    g = math.gcd(w, hn)
    span = 2 * hn
    m = span // half
    me = lax.axis_index("seq")
    plane = me // GROUP
    r = me % GROUP
    y = r // 2
    c = r % 2
    core_peer = plane * GROUP + y * 2 + (1 - c)
    pair_peer = plane * GROUP + (1 - y) * 2 + c

    def send(src, dst, ss, rs, dev):
        return pltpu.make_async_remote_copy(
            src_ref=src, dst_ref=dst, send_sem=ss, recv_sem=rs,
            device_id={"seq": dev}, device_id_type=MESH,
        )

    def head0(j, yh):
        return (j // m) * (2 * span) + yh * span + (j % m) * half

    def hcol(j, yh, hh):
        return pl.ds(pl.multiple_of((head0(j, yh) + hh) * D, D), D)

    k_s, v_s = kv_s.at[0], kv_s.at[1]
    q_s, g_s = qg_s.at[0], qg_s.at[1]

    def fetch(first, second, both):
        def go(p, carry):
            for yh in range(2):
                at = pl.ds(pl.multiple_of(head0(p * per, yh) * D, half * per * D), half * per * D)
                pltpu.make_async_copy(first.at[:, at], both.at[0, :, at], load_sem.at[p]).start()
                pltpu.make_async_copy(second.at[:, at], both.at[1, :, at], load_sem.at[p]).start()
            return carry
        return go

    def fetched(both, sem, p):
        part = both.at[:, :, pl.ds(0, 2 * half * per * D)]
        pltpu.make_async_copy(part, part, sem.at[p]).wait()

    ld_copy = pltpu.make_async_copy(ld_hbm, ld_s.at[pl.ds(0, heads)], small_sem.at[0])
    docs_copy = pltpu.make_async_copy(docs_hbm, docs_s, small_sem.at[1])
    gain_copy = pltpu.make_async_copy(gain_hbm, gain_s, small_sem.at[2])
    ld_copy.start()
    docs_copy.start()
    barrier = pltpu.get_barrier_semaphore()
    for d in range(1, GROUP):
        pl.semaphore_signal(
            barrier, inc=1, device_id={"seq": plane * GROUP + (r + d) % GROUP}, device_id_type=MESH
        )

    @pl.when(plane > 0)
    def _():
        pl.semaphore_signal(barrier, inc=1, device_id={"seq": me - GROUP}, device_id_type=MESH)

    lax.fori_loop(0, AHEAD, fetch(k_hbm, v_hbm, kv_s), 0)

    gain_copy.start()

    if heads < D:
        ld_s[pl.ds(heads, D - heads)] = jnp.zeros((D - heads, tok), BF16)
    base = me * tok
    row_i = lax.broadcasted_iota(jnp.int32, (tok, tok), 0)
    col_i = lax.broadcasted_iota(jnp.int32, (tok, tok), 1)
    causal = row_i >= col_i
    lanes = lax.broadcasted_iota(jnp.int32, (1, tok), 1)
    docs_copy.wait()
    n_docs = docs_s.shape[0]
    doc_row = jnp.zeros((1, tok), jnp.int32)
    before = jnp.int32(0)
    last = jnp.int32(0)
    end = jnp.int32(0)
    for d in range(n_docs):
        end = end + docs_s[d]
        doc_row = doc_row + jnp.where(lanes + base >= end, 1, 0)
        before = before + jnp.where(base - 1 >= end, 1, 0)
        last = last + jnp.where(base + tok - 1 >= end, 1, 0)
    closing = jnp.where(doc_row == last, 1.0, 0.0).astype(F32)
    ld_copy.wait()
    upper = jnp.where(row_i <= col_i, 1.0, 0.0).astype(BF16)
    cumt = dot(ld_s[pl.ds(0, heads)], upper, ((1,), (0,)))
    cumt_s[...] = LOG2E * cumt
    total = cumt[:, tok - 1:tok]
    kwt_s[...] = closing * jnp.exp(total - cumt)

    def updates(u):
        fetched(kv_s, load_sem, u)
        fetch(q_hbm, g_hbm, qg_s)(u, 0)

        @pl.when(u + AHEAD < loads)
        def _():
            fetch(k_hbm, v_hbm, kv_s)(u + AHEAD, 0)

    def update_math(j):
        for yh in range(2):
            for hh in range(half):
                h = head0(j, yh) + hh
                kt = k_s[:, hcol(j, yh, hh)].T
                kt_s[h] = kt
                wk = (kt.astype(F32) * kwt_s[pl.ds(h, 1), :]).astype(BF16)
                up = dot(wk, v_s[:, hcol(j, yh, hh)], ((1,), (0,)))
                u_own[j, hh // w, yh, hh % w] = up.astype(BF16)

    def core_copy(j):
        return send(u_own.at[j, 1 - c], u_core.at[j], core_ss, core_rs.at[j], core_peer)

    def pair_copy(j):
        return send(u_send.at[j], u_pair.at[j], pair_ss, pair_rs.at[j], pair_peer)

    def z_copy(j):
        return send(s_out.at[j], s_in.at[j], z_ss, z_rs.at[j], (me + GROUP) % n)

    def e_copy(j):
        return send(e_send.at[j], e_half.at[j, y], e_ss, e_rs.at[j], pair_peer)

    def x_copy(j):
        at = pl.ds(j * per, per)
        return send(x_send.at[at], ent.at[at, c], x_ss, x_rs.at[j], core_peer)

    def fac_core_copy():
        return send(fac_own, fac_core, fac_ss.at[0], fac_rs.at[0], core_peer)

    def fac_pair_copy():
        return send(fac_chip.at[c, 1 - y], fac_pair, fac_ss.at[1], fac_rs.at[1], pair_peer)

    def combine(j):
        core_copy(j).wait_recv()
        for k in range(w):
            for yo in range(2):
                at = pl.ds(j * w + k, 1)
                fa = jnp.where(c == 0, fac_core[c, yo, at, :], 1.0)
                fb = jnp.where(c == 0, 1.0, fac_own[c, yo, at, :])
                val = fa * u_own[j, c, yo, k].astype(F32) + fb * u_core[j, yo, k].astype(F32)

                @pl.when(yo == y)
                def _():
                    u_mine[j, k] = val

                @pl.when(yo != y)
                def _():
                    u_send[j, k] = val.astype(BF16)
        pair_copy(j).start()

    def fin_place(j, s):
        h = head0(j, y) + c * w + s * g
        return h // hn, h % hn

    def fin_copy(j, s):
        dev, off = fin_place(j, s)
        return send(
            s_out.at[j, pl.ds(s * g, g)], fin_s.at[pl.ds(off, g)],
            f_ss, f_rs.at[off // g], dev,
        )

    def fin_local(j, s):
        _, off = fin_place(j, s)
        return pltpu.make_async_copy(s_out.at[j, pl.ds(s * g, g)], fin_s.at[pl.ds(off, g)], f_ls)

    def chain(j):
        @pl.when(j == 0)
        def _():
            fac_pair_copy().wait_recv()

        pair_copy(j).wait_recv()

        @pl.when(plane > 0)
        def _():
            z_copy(j).wait_recv()

        for k in range(w):
            at = pl.ds(j * w + k, 1)
            chip = fac_chip[c, y, at, :]
            other_chip = fac_pair[at, :]
            f01 = jnp.where(y == 0, chip, other_chip)
            f23 = jnp.where(y == 0, other_chip, chip)
            mine = u_mine[j, k]
            other = u_pair[j, k].astype(F32)
            entry = s_in[j, k].astype(F32)
            mid = f01 * entry + jnp.where(y == 0, mine, other)
            s_out[j, k] = (f23 * mid + jnp.where(y == 0, other, mine)).astype(BF16)
            e_send[j, k] = jnp.where(y == 0, mid, entry).astype(BF16)
            e_half[j, y, k] = jnp.where(y == 0, entry, mid).astype(BF16)

        @pl.when(plane < planes - 1)
        def _():
            z_copy(j).start()

        @pl.when(plane == planes - 1)
        def _():
            for s in range(w // g):
                dev, _off = fin_place(j, s)

                @pl.when(dev != me)
                def _():
                    fin_copy(j, s).start()

                @pl.when(dev == me)
                def _():
                    fin_local(j, s).start()
                    fin_local(j, s).wait()

    def inside_wait(i):
        @pl.when((i % 2 == 0) & (i < 2 * loads))
        def _():
            fetched(qg_s, load_sem, i // 2)

    def place(i):
        j = (i // 2) * per
        return j, i % 2, head0(j, i % 2)

    def wide(j, yh, hh):
        return pl.ds(pl.multiple_of((head0(j, yh) + hh) * D, 2 * D), 2 * D)

    def weigh(i):
        j, yh, h0 = place(i)
        blk = tok // 2
        cols = pltpu.roll(cum_s[...], (D - h0) % D, 1)
        for hh in range(0, half * per, 2):
            top = dot(
                q_s[:blk, wide(j, yh, hh)],
                diagonal(kt_s[h0 + hh, :, :blk], kt_s[h0 + hh + 1, :, :blk]), ((1,), (0,)),
            )
            for b in range(2):
                h = hh + b
                row = cumt_s[pl.ds(h0 + h, 1), :]
                ci = cols[:, h:h + 1]
                bot = dot(q_s[blk:, hcol(j, yh, h)], kt_s[h0 + h], ((1,), (0,)))
                at = slice(b * blk, (b + 1) * blk)
                wt_s[hh // 2, 0, :, at] = (
                    top[:, at] * jnp.exp2((ci[:blk] - row[:, :blk]) + pen_s[:blk, :blk])
                ).astype(BF16)
                wt_s[hh // 2, 1 + b] = (bot * jnp.exp2((ci[blk:] - row) + pen_s[blk:, :])).astype(BF16)

    def apply(i):
        j, yh, h0 = place(i)
        blk = tok // 2
        for hh in range(0, half * per, 2):
            both = wide(j, yh, hh)
            mix_s[:blk, both] = dot(
                wt_s[hh // 2, 0],
                diagonal(v_s[:blk, hcol(j, yh, hh)], v_s[:blk, hcol(j, yh, hh + 1)]), ((1,), (0,)),
            )
            for b in range(2):
                at = hcol(j, yh, hh + b)
                mix_s[blk:, at] = dot(wt_s[hh // 2, 1 + b], v_s[:, at], ((1,), (0,)))
            hg = 0.5 * gain_s[:, both]
            gate_s[:, both] = hg * jnp.tanh(0.5 * g_s[:, both].astype(F32)) + hg

    def share(j):
        @pl.when((plane > 0) | (y == 0))
        def _():
            e_copy(j).start()

    def spread(j):
        @pl.when((plane > 0) | (y == 1))
        def _():
            e_copy(j).wait_recv()

        for yo in range(2):
            for k in range(w):
                at = pl.ds(j * w + k, 1)
                f0 = jnp.where(c == 0, fac_own[c, yo, at, :], fac_core[c, yo, at, :])
                first = e_half[j, yo, k]
                u0 = jnp.where(c == 0, u_own[j, 0, yo, k], u_core[j, yo, k]).astype(F32)
                second = (f0 * first.astype(F32) + u0).astype(BF16)
                ent[j, c, yo, k] = jnp.where(c == 0, first, second)
                x_send[j, yo, k] = jnp.where(c == 0, second, first)

        @pl.when(j % per == per - 1)
        def _():
            x_copy(j // per).start()

    def across_wait(a):
        x_copy(a).wait_recv()

    def across(a):
        j = a * per
        cols = pltpu.roll(lead_s[...], (D - head0(j, 0)) % D, 1)
        acc = ssq_s[...]
        for yh in range(2):
            for hh in range(0, half * per, 2):
                entry = [ent[j + h // half, (h % half) // w, yh, h % w] for h in (hh, hh + 1)]
                both = dot(q_s[:, wide(j, yh, hh)], diagonal(*entry), ((1,), (0,)))
                for b in range(2):
                    at = hcol(j, yh, hh + b)
                    lane = yh * span + hh + b
                    mixed = mix_s[:, at] + cols[:, lane:lane + 1] * both[:, b * D:(b + 1) * D]
                    acc = acc + mixed * mixed
                    out_s[:, at] = (mixed * gate_s[:, at]).astype(BF16)
        ssq_s[...] = acc

    updates(0)
    update_math(0)
    own_f = jnp.where(last == before, 1.0, 0.0).astype(F32) * jnp.exp(jnp.broadcast_to(total, (heads, D)))
    for j in range(chunks):
        for yh in range(2):
            for cc in range(2):
                h = head0(j, yh) + cc * w
                fac_own[cc, yh, j * w:(j + 1) * w, :] = own_f[h:h + w]

    @pl.when(plane < planes - 1)
    def _():
        pl.semaphore_wait(barrier, GROUP)

    @pl.when(plane == planes - 1)
    def _():
        pl.semaphore_wait(barrier, GROUP - 1)

    core_copy(0).start()
    fac_core_copy().start()
    for j in range(1, per):
        update_math(j)
        core_copy(j).start()
    updates(1)
    for j in range(per, 2 * per):
        update_math(j)
        core_copy(j).start()
    fac_core_copy().wait_recv()
    fac_chip[...] = fac_own[...] * fac_core[...]
    fac_pair_copy().start()
    for j in range(per):
        combine(j)

    rows = lax.broadcasted_iota(jnp.int32, (tok, D), 0)
    doc_col = jnp.zeros((tok, D), jnp.int32)
    end = jnp.int32(0)
    for d in range(n_docs):
        end = end + docs_s[d]
        doc_col = doc_col + jnp.where(rows + base >= end, 1, 0)
    pen_s[...] = jnp.where(causal & (doc_col[:, :1] == doc_row), 0.0, -1e30).astype(F32)
    tri = jnp.where(causal, 1.0, 0.0).astype(BF16)
    cum = dot(tri, ld_s[...], ((1,), (1,)))
    cum_s[...] = LOG2E * cum
    lead_s[...] = jnp.where(doc_col == before, 1.0, 0.0).astype(F32) * jnp.exp(cum)
    ssq_s[...] = jnp.zeros_like(ssq_s)

    @pl.when(plane == 0)
    def _():
        s_in[...] = jnp.zeros_like(s_in)

    @pl.when((plane == 0) & (y == 0))
    def _():
        e_half[:, 1] = jnp.zeros(e_half.shape[:1] + e_half.shape[2:], BF16)

    gain_copy.wait()
    for j in range(per, 2 * per):
        combine(j)
    updates(2)
    inside_wait(0)
    for j in range(2 * per, 3 * per):
        update_math(j)
    weigh(0)
    for j in range(2 * per, 3 * per):
        core_copy(j).start()

    chain_lag = 9 + 4 * plane + 2 * (plane // (planes - 1))
    e_lag = jnp.maximum(chain_lag, chunks + per + 1)
    ends = jnp.where(plane == planes - 1, 0, chain_lag + chunks - SPREAD_EARLY)
    spread_lag = jnp.maximum(e_lag + E_LAG, ends)
    across_lag = (spread_lag + X_LAG + 2) // 2 * 2 + 1
    steps = jnp.maximum(across_lag + chunks, (2 * loads + 3) * per)

    def step(t, carry):
        def at(lag, count, body, first=0):
            @pl.when((t >= lag + first) & (t < lag + count))
            def _():
                body(t - lag)

        at(per + 1, chunks, combine, 2 * per)
        at(chain_lag, chunks, chain)
        at(e_lag, chunks, share)
        at(spread_lag, chunks, spread)

        u = t // per
        a = (t - across_lag) // per
        even = t % per == 0
        odd = t % per == 1
        states = odd & (t >= across_lag) & (t < across_lag + chunks)

        @pl.when(even & (u < loads))
        def _():
            updates(u)
            inside_wait(u - 2)
            for j in range(per):
                update_math(t + j)
            apply(u - 3)
            weigh(u - 2)
            for j in range(per):
                core_copy(t + j).start()

        i = t - chunks + loads - 2

        @pl.when((t >= chunks) & (i < 2 * loads))
        def _():
            inside_wait(i)
            apply(i - 1)
            weigh(i)

        @pl.when(i == 2 * loads)
        def _():
            apply(i - 1)

        @pl.when(states)
        def _():
            across_wait(a)
            across(a)

        return carry

    lax.fori_loop(3 * per, steps, step, 0)

    mean = jnp.sum(ssq_s[...], axis=1, keepdims=True) * (1.0 / (heads * D))
    ssq_s[...] = jnp.broadcast_to(lax.rsqrt(mean + EPS), (tok, D))

    for s in range(hn // g):
        h = me * hn + s * g
        src = (planes - 1) * GROUP + ((h // span) % 2) * 2 + (h % half) // w

        @pl.when(src != me)
        def _():
            send(
                s_out.at[0, pl.ds(0, g)], fin_s.at[pl.ds(s * g, g)], f_ss, f_rs.at[s], core_peer
            ).wait_recv()

    fac_core_copy().wait_send()
    fac_pair_copy().wait_send()
    send(u_own.at[:, 1 - c], u_core, core_ss, core_rs.at[0], core_peer).wait_send()
    send(u_send, u_pair, pair_ss, pair_rs.at[0], pair_peer).wait_send()

    @pl.when((plane > 0) | (y == 0))
    def _():
        send(e_send, s_in, e_ss, e_rs.at[0], pair_peer).wait_send()

    send(x_send, e_half, x_ss, x_rs.at[0], core_peer).wait_send()

    @pl.when(plane < planes - 1)
    def _():
        send(s_out, s_in, z_ss, z_rs.at[0], (me + GROUP) % n).wait_send()

    @pl.when(plane == planes - 1)
    def _():
        sent = pl.ds(0, chunks - max(1, hn // (2 * w)))
        send(s_out.at[sent], s_in.at[sent], f_ss, f_rs.at[0], core_peer).wait_send()


def finish_kernel(mix_ref, inv_ref, fin_in, out_hbm, fin_hbm, buf, fin_s, sem, fin_sem):
    parts = buf.shape[0]
    rows = buf.shape[1]
    fin_s[...] = fin_in[...].astype(F32)
    fin_copy = pltpu.make_async_copy(fin_s, fin_hbm, fin_sem)
    fin_copy.start()
    copies = [fin_copy]
    for p in range(parts):
        at = slice(p * rows, (p + 1) * rows)
        inv = inv_ref[at, :]
        for t in range(mix_ref.shape[1] // D):
            cols = slice(t * D, (t + 1) * D)
            buf[p, :, cols] = (mix_ref[at, cols].astype(F32) * inv).astype(BF16)
        copy = pltpu.make_async_copy(buf.at[p], out_hbm.at[pl.ds(p * rows, rows)], sem.at[p])
        copy.start()
        copies.append(copy)
    for copy in copies:
        copy.wait()


def shards(n, queries, keys_in, values_in, log_decay, gate_logits, norm_gain, doc_lengths):
    tok, width = queries.shape
    heads = width // D
    chunks = CHUNKS
    hc = heads // chunks
    half = hc // 2
    w = half // 2
    hn = heads // n
    g = math.gcd(w, hn)
    vm = pltpu.VMEM
    dma = pltpu.SemaphoreType.DMA
    anyspace = pl.BlockSpec(memory_space=pl.ANY)
    vspec = pl.BlockSpec(memory_space=pltpu.VMEM)
    part = vm((chunks, w, D, D), BF16)
    fac = vm((2, 2, chunks * w, D), F32)
    scratch = [
        vm((tok, width), F32), vm((tok, width), F32),
        vm((2, tok, width), BF16), vm((2, tok, width), BF16),
        vm((heads, D, tok), BF16), vm((max(heads, D), tok), BF16), vm((1, width), F32),
        pltpu.SMEM(doc_lengths.shape, jnp.int32),
        vm((tok, tok), F32), vm((heads, tok), F32), vm((heads, tok), F32), vm((tok, D), F32), vm((tok, D), F32),
        fac, fac, fac, vm((chunks * w, D), F32),
        vm((hc // 4 * (chunks // LOADS), 3, tok // 2, tok), BF16),
        vm((chunks, 2, 2, w, D, D), BF16), vm((chunks, 2, w, D, D), BF16), vm((chunks, w, D, D), F32),
        part, part, part, part, part,
        vm((chunks, 2, w, D, D), BF16), vm((chunks, 2, w, D, D), BF16),
        vm((chunks, 2, 2, w, D, D), BF16),
        dma((LOADS,)), dma((3,)), dma((2,)), dma((2,)),
        dma, dma((chunks,)), dma, dma((chunks,)), dma, dma((chunks,)), dma, dma((chunks,)), dma, dma((LOADS,)),
        dma, dma((hn // g,)), dma,
    ]
    mixed, squares, final = pl.pallas_call(
        functools.partial(kernel, n, heads, chunks),
        out_shape=(
            pltpu.VMEM((tok, width), BF16),
            pltpu.VMEM((tok, D), F32),
            pltpu.VMEM((hn, D, D), BF16),
        ),
        in_specs=[anyspace] * 7,
        out_specs=(vspec, vspec, vspec),
        scratch_shapes=scratch,
        compiler_params=pltpu.CompilerParams(
            collective_id=0, has_side_effects=True, vmem_limit_bytes=54 * 1024 * 1024
        ),
    )(queries, keys_in, values_in, gate_logits, log_decay.T, norm_gain.reshape(1, width), doc_lengths)
    rows = tok // FINISH_PARTS
    return pl.pallas_call(
        finish_kernel,
        out_shape=(
            jax.ShapeDtypeStruct((tok, width), BF16),
            jax.ShapeDtypeStruct((hn, D, D), F32),
        ),
        in_specs=[vspec, vspec, vspec],
        out_specs=(anyspace, anyspace),
        scratch_shapes=[
            vm((FINISH_PARTS, rows, width), BF16), vm((hn, D, D), F32), dma((FINISH_PARTS,)), dma,
        ],
        compiler_params=pltpu.CompilerParams(vmem_limit_bytes=16 * 1024 * 1024),
    )(mixed, squares, final)


def solution(mesh):
    rows = P(("grp", "seq"), None)
    return jax.shard_map(
        functools.partial(shards, mesh.shape["seq"]),
        mesh=mesh,
        in_specs=(rows, rows, rows, rows, rows, P(), P("grp")),
        out_specs=(rows, P(("grp", "seq"), None, None)),
        check_vma=False,
    )
```

```python
import functools
import math

import jax
import jax.numpy as jnp
from jax import lax
from jax.experimental import pallas as pl
from jax.experimental.pallas import tpu as pltpu
from jax.sharding import PartitionSpec as P

EPS = 1e-05
LOG2E = 1.4426950408889634
D = 128
GROUP = 4
CHUNKS = 16
LOADS = 8
AHEAD = 2
CHAIN_LAG = 9
HOP_LAG = 4
E_LAG = 5
X_LAG = 1
SPREAD_EARLY = 8
FINISH_PARTS = 8
F32, BF16 = jnp.float32, jnp.bfloat16
MESH = pl.DeviceIdType.MESH


def dot(a, b, dims):
    return lax.dot_general(a, b, (dims, ((), ())), preferred_element_type=F32)


def diagonal(a, b):
    zero = jnp.zeros_like(a)
    return jnp.concatenate([jnp.concatenate([a, zero], axis=1), jnp.concatenate([zero, b], axis=1)], axis=0)


def kernel(
    n, heads, chunks,
    q_hbm, k_hbm, v_hbm, g_hbm, ld_hbm, gain_hbm, docs_hbm,
    out_s, ssq_s, fin_s,
    mix_s, gate_s, kv_s, qg_s, kt_s, ld_s, gain_s, docs_s, pen_s, cumt_s, kwt_s, cum_s, lead_s,
    fac_own, fac_core, fac_chip, fac_pair, wt_s, u_own, u_core, u_mine, u_send, u_pair, s_in, s_out, e_send, e_half,
    x_send, ent,
    load_sem, small_sem, fac_ss, fac_rs, core_ss, core_rs, pair_ss, pair_rs, z_ss, z_rs, e_ss, e_rs,
    x_ss, x_rs, f_ss, f_rs, f_ls,
):
    tok = q_hbm.shape[0]
    hc = heads // chunks
    half = hc // 2
    w = half // 2
    planes = n // GROUP
    loads = LOADS
    per = chunks // loads
    hn = heads // n
    g = math.gcd(w, hn)
    span = 2 * hn
    m = span // half
    me = lax.axis_index("seq")
    plane = me // GROUP
    r = me % GROUP
    y = r // 2
    c = r % 2
    core_peer = plane * GROUP + y * 2 + (1 - c)
    pair_peer = plane * GROUP + (1 - y) * 2 + c

    def send(src, dst, ss, rs, dev):
        return pltpu.make_async_remote_copy(
            src_ref=src, dst_ref=dst, send_sem=ss, recv_sem=rs,
            device_id={"seq": dev}, device_id_type=MESH,
        )

    def head0(j, yh):
        return (j // m) * (2 * span) + yh * span + (j % m) * half

    def hcol(j, yh, hh):
        return pl.ds(pl.multiple_of((head0(j, yh) + hh) * D, D), D)

    k_s, v_s = kv_s.at[0], kv_s.at[1]
    q_s, g_s = qg_s.at[0], qg_s.at[1]

    def fetch(first, second, both):
        def go(p, carry):
            for yh in range(2):
                at = pl.ds(pl.multiple_of(head0(p * per, yh) * D, half * per * D), half * per * D)
                pltpu.make_async_copy(first.at[:, at], both.at[0, :, at], load_sem.at[p]).start()
                pltpu.make_async_copy(second.at[:, at], both.at[1, :, at], load_sem.at[p]).start()
            return carry
        return go

    def fetched(both, sem, p):
        part = both.at[:, :, pl.ds(0, 2 * half * per * D)]
        pltpu.make_async_copy(part, part, sem.at[p]).wait()

    ld_copy = pltpu.make_async_copy(ld_hbm, ld_s.at[pl.ds(0, heads)], small_sem.at[0])
    docs_copy = pltpu.make_async_copy(docs_hbm, docs_s, small_sem.at[1])
    gain_copy = pltpu.make_async_copy(gain_hbm, gain_s, small_sem.at[2])
    ld_copy.start()
    docs_copy.start()
    barrier = pltpu.get_barrier_semaphore()
    for d in range(1, GROUP):
        pl.semaphore_signal(
            barrier, inc=1, device_id={"seq": plane * GROUP + (r + d) % GROUP}, device_id_type=MESH
        )

    @pl.when(plane > 0)
    def _():
        pl.semaphore_signal(barrier, inc=1, device_id={"seq": me - GROUP}, device_id_type=MESH)

    lax.fori_loop(0, AHEAD, fetch(k_hbm, v_hbm, kv_s), 0)

    gain_copy.start()

    if heads < D:
        ld_s[pl.ds(heads, D - heads)] = jnp.zeros((D - heads, tok), BF16)
    base = me * tok
    row_i = lax.broadcasted_iota(jnp.int32, (tok, tok), 0)
    col_i = lax.broadcasted_iota(jnp.int32, (tok, tok), 1)
    causal = row_i >= col_i
    lanes = lax.broadcasted_iota(jnp.int32, (1, tok), 1)
    docs_copy.wait()
    n_docs = docs_s.shape[0]
    doc_row = jnp.zeros((1, tok), jnp.int32)
    before = jnp.int32(0)
    last = jnp.int32(0)
    end = jnp.int32(0)
    for d in range(n_docs):
        end = end + docs_s[d]
        doc_row = doc_row + jnp.where(lanes + base >= end, 1, 0)
        before = before + jnp.where(base - 1 >= end, 1, 0)
        last = last + jnp.where(base + tok - 1 >= end, 1, 0)
    closing = jnp.where(doc_row == last, 1.0, 0.0).astype(F32)
    ld_copy.wait()
    upper = jnp.where(row_i <= col_i, 1.0, 0.0).astype(BF16)
    cumt = dot(ld_s[pl.ds(0, heads)], upper, ((1,), (0,)))
    cumt_s[...] = LOG2E * cumt
    total = cumt[:, tok - 1:tok]
    kwt_s[...] = closing * jnp.exp(total - cumt)

    def updates(u):
        fetched(kv_s, load_sem, u)
        fetch(q_hbm, g_hbm, qg_s)(u, 0)

        @pl.when(u + AHEAD < loads)
        def _():
            fetch(k_hbm, v_hbm, kv_s)(u + AHEAD, 0)

    def update_math(j):
        for yh in range(2):
            for hh in range(half):
                h = head0(j, yh) + hh
                kt = k_s[:, hcol(j, yh, hh)].T
                kt_s[h] = kt
                wk = (kt.astype(F32) * kwt_s[pl.ds(h, 1), :]).astype(BF16)
                up = dot(wk, v_s[:, hcol(j, yh, hh)], ((1,), (0,)))
                u_own[j, hh // w, yh, hh % w] = up.astype(BF16)

    def core_copy(j):
        return send(u_own.at[j, 1 - c], u_core.at[j], core_ss, core_rs.at[j], core_peer)

    def pair_copy(j):
        return send(u_send.at[j], u_pair.at[j], pair_ss, pair_rs.at[j], pair_peer)

    def z_copy(j):
        return send(s_out.at[j], s_in.at[j], z_ss, z_rs.at[j], (me + GROUP) % n)

    def e_copy(j):
        return send(e_send.at[j], e_half.at[j, y], e_ss, e_rs.at[j], pair_peer)

    def x_copy(j):
        at = pl.ds(j * per, per)
        return send(x_send.at[at], ent.at[at, c], x_ss, x_rs.at[j], core_peer)

    def fac_core_copy():
        return send(fac_own, fac_core, fac_ss.at[0], fac_rs.at[0], core_peer)

    def fac_pair_copy():
        return send(fac_chip.at[c, 1 - y], fac_pair, fac_ss.at[1], fac_rs.at[1], pair_peer)

    def combine(j):
        core_copy(j).wait_recv()
        for k in range(w):
            for yo in range(2):
                at = pl.ds(j * w + k, 1)
                fa = jnp.where(c == 0, fac_core[c, yo, at, :], 1.0)
                fb = jnp.where(c == 0, 1.0, fac_own[c, yo, at, :])
                val = fa * u_own[j, c, yo, k].astype(F32) + fb * u_core[j, yo, k].astype(F32)

                @pl.when(yo == y)
                def _():
                    u_mine[j, k] = val

                @pl.when(yo != y)
                def _():
                    u_send[j, k] = val.astype(BF16)
        pair_copy(j).start()

    def fin_place(j, s):
        h = head0(j, y) + c * w + s * g
        return h // hn, h % hn

    def fin_copy(j, s):
        dev, off = fin_place(j, s)
        return send(
            s_out.at[j, pl.ds(s * g, g)], fin_s.at[pl.ds(off, g)],
            f_ss, f_rs.at[off // g], dev,
        )

    def fin_local(j, s):
        _, off = fin_place(j, s)
        return pltpu.make_async_copy(s_out.at[j, pl.ds(s * g, g)], fin_s.at[pl.ds(off, g)], f_ls)

    def chain(j):
        @pl.when(j == 0)
        def _():
            fac_pair_copy().wait_recv()

        pair_copy(j).wait_recv()

        @pl.when(plane > 0)
        def _():
            z_copy(j).wait_recv()

        for k in range(w):
            at = pl.ds(j * w + k, 1)
            chip = fac_chip[c, y, at, :]
            other_chip = fac_pair[at, :]
            f01 = jnp.where(y == 0, chip, other_chip)
            f23 = jnp.where(y == 0, other_chip, chip)
            mine = u_mine[j, k]
            other = u_pair[j, k].astype(F32)
            entry = s_in[j, k].astype(F32)
            mid = f01 * entry + jnp.where(y == 0, mine, other)
            s_out[j, k] = (f23 * mid + jnp.where(y == 0, other, mine)).astype(BF16)
            e_send[j, k] = jnp.where(y == 0, mid, entry).astype(BF16)
            e_half[j, y, k] = jnp.where(y == 0, entry, mid).astype(BF16)

        @pl.when(plane < planes - 1)
        def _():
            z_copy(j).start()

        @pl.when(plane == planes - 1)
        def _():
            for s in range(w // g):
                dev, _off = fin_place(j, s)

                @pl.when(dev != me)
                def _():
                    fin_copy(j, s).start()

                @pl.when(dev == me)
                def _():
                    fin_local(j, s).start()
                    fin_local(j, s).wait()

    def inside_wait(i):
        @pl.when((i % 2 == 0) & (i < 2 * loads))
        def _():
            fetched(qg_s, load_sem, i // 2)

    def place(i):
        j = (i // 2) * per
        return j, i % 2, head0(j, i % 2)

    def wide(j, yh, hh):
        return pl.ds(pl.multiple_of((head0(j, yh) + hh) * D, 2 * D), 2 * D)

    def weigh(i):
        j, yh, h0 = place(i)
        blk = tok // 2
        cols = pltpu.roll(cum_s[...], (D - h0) % D, 1)
        for hh in range(0, half * per, 2):
            top = dot(
                q_s[:blk, wide(j, yh, hh)],
                diagonal(kt_s[h0 + hh, :, :blk], kt_s[h0 + hh + 1, :, :blk]), ((1,), (0,)),
            )
            for b in range(2):
                h = hh + b
                row = cumt_s[pl.ds(h0 + h, 1), :]
                ci = cols[:, h:h + 1]
                bot = dot(q_s[blk:, hcol(j, yh, h)], kt_s[h0 + h], ((1,), (0,)))
                at = slice(b * blk, (b + 1) * blk)
                wt_s[hh // 2, 0, :, at] = (
                    top[:, at] * jnp.exp2((ci[:blk] - row[:, :blk]) + pen_s[:blk, :blk])
                ).astype(BF16)
                wt_s[hh // 2, 1 + b] = (bot * jnp.exp2((ci[blk:] - row) + pen_s[blk:, :])).astype(BF16)

    def apply(i):
        j, yh, h0 = place(i)
        blk = tok // 2
        for hh in range(0, half * per, 2):
            both = wide(j, yh, hh)
            mix_s[:blk, both] = dot(
                wt_s[hh // 2, 0],
                diagonal(v_s[:blk, hcol(j, yh, hh)], v_s[:blk, hcol(j, yh, hh + 1)]), ((1,), (0,)),
            )
            for b in range(2):
                at = hcol(j, yh, hh + b)
                mix_s[blk:, at] = dot(wt_s[hh // 2, 1 + b], v_s[:, at], ((1,), (0,)))
            hg = 0.5 * gain_s[:, both]
            gate_s[:, both] = hg * jnp.tanh(0.5 * g_s[:, both].astype(F32)) + hg

    def share(j):
        @pl.when((plane > 0) | (y == 0))
        def _():
            e_copy(j).start()

    def spread(j):
        @pl.when((plane > 0) | (y == 1))
        def _():
            e_copy(j).wait_recv()

        for yo in range(2):
            for k in range(w):
                at = pl.ds(j * w + k, 1)
                f0 = jnp.where(c == 0, fac_own[c, yo, at, :], fac_core[c, yo, at, :])
                first = e_half[j, yo, k]
                u0 = jnp.where(c == 0, u_own[j, 0, yo, k], u_core[j, yo, k]).astype(F32)
                second = (f0 * first.astype(F32) + u0).astype(BF16)
                ent[j, c, yo, k] = jnp.where(c == 0, first, second)
                x_send[j, yo, k] = jnp.where(c == 0, second, first)

        @pl.when(j % per == per - 1)
        def _():
            x_copy(j // per).start()

    def across_wait(a):
        x_copy(a).wait_recv()

    def across(a):
        j = a * per
        cols = pltpu.roll(lead_s[...], (D - head0(j, 0)) % D, 1)
        acc = ssq_s[...]
        for yh in range(2):
            for hh in range(0, half * per, 2):
                entry = [ent[j + h // half, (h % half) // w, yh, h % w] for h in (hh, hh + 1)]
                both = dot(q_s[:, wide(j, yh, hh)], diagonal(*entry), ((1,), (0,)))
                for b in range(2):
                    at = hcol(j, yh, hh + b)
                    lane = yh * span + hh + b
                    mixed = mix_s[:, at] + cols[:, lane:lane + 1] * both[:, b * D:(b + 1) * D]
                    acc = acc + mixed * mixed
                    out_s[:, at] = (mixed * gate_s[:, at]).astype(BF16)
        ssq_s[...] = acc

    updates(0)
    update_math(0)
    own_f = jnp.where(last == before, 1.0, 0.0).astype(F32) * jnp.exp(jnp.broadcast_to(total, (heads, D)))
    for j in range(chunks):
        for yh in range(2):
            for cc in range(2):
                h = head0(j, yh) + cc * w
                fac_own[cc, yh, j * w:(j + 1) * w, :] = own_f[h:h + w]

    @pl.when(plane < planes - 1)
    def _():
        pl.semaphore_wait(barrier, GROUP)

    @pl.when(plane == planes - 1)
    def _():
        pl.semaphore_wait(barrier, GROUP - 1)

    core_copy(0).start()
    fac_core_copy().start()
    for j in range(1, per):
        update_math(j)
        core_copy(j).start()
    updates(1)
    for j in range(per, 2 * per):
        update_math(j)
        core_copy(j).start()
    fac_core_copy().wait_recv()
    fac_chip[...] = fac_own[...] * fac_core[...]
    fac_pair_copy().start()
    for j in range(per):
        combine(j)

    rows = lax.broadcasted_iota(jnp.int32, (tok, D), 0)
    doc_col = jnp.zeros((tok, D), jnp.int32)
    end = jnp.int32(0)
    for d in range(n_docs):
        end = end + docs_s[d]
        doc_col = doc_col + jnp.where(rows + base >= end, 1, 0)
    pen_s[...] = jnp.where(causal & (doc_col[:, :1] == doc_row), 0.0, -1e30).astype(F32)
    tri = jnp.where(causal, 1.0, 0.0).astype(BF16)
    cum = dot(tri, ld_s[...], ((1,), (1,)))
    cum_s[...] = LOG2E * cum
    lead_s[...] = jnp.where(doc_col == before, 1.0, 0.0).astype(F32) * jnp.exp(cum)
    ssq_s[...] = jnp.zeros_like(ssq_s)

    @pl.when(plane == 0)
    def _():
        s_in[...] = jnp.zeros_like(s_in)

    @pl.when((plane == 0) & (y == 0))
    def _():
        e_half[:, 1] = jnp.zeros(e_half.shape[:1] + e_half.shape[2:], BF16)

    gain_copy.wait()
    for j in range(per, 2 * per):
        combine(j)
    updates(2)
    inside_wait(0)
    for j in range(2 * per, 3 * per):
        update_math(j)
    weigh(0)
    for j in range(2 * per, 3 * per):
        core_copy(j).start()

    chain_lag = 9 + 4 * plane + 2 * (plane // (planes - 1))
    e_lag = jnp.maximum(chain_lag, chunks + per + 1)
    ends = jnp.where(plane == planes - 1, 0, chain_lag + chunks - SPREAD_EARLY)
    spread_lag = jnp.maximum(e_lag + E_LAG, ends)
    across_lag = (spread_lag + X_LAG + 2) // 2 * 2 + 1
    steps = jnp.maximum(across_lag + chunks, (2 * loads + 3) * per)

    def step(t, carry):
        def at(lag, count, body, first=0):
            @pl.when((t >= lag + first) & (t < lag + count))
            def _():
                body(t - lag)

        at(per + 1, chunks, combine, 2 * per)
        at(chain_lag, chunks, chain)
        at(e_lag, chunks, share)
        at(spread_lag, chunks, spread)

        u = t // per
        a = (t - across_lag) // per
        even = t % per == 0
        odd = t % per == 1
        states = odd & (t >= across_lag) & (t < across_lag + chunks)

        @pl.when(even & (u < loads))
        def _():
            updates(u)
            inside_wait(u - 2)
            for j in range(per):
                update_math(t + j)
            apply(u - 3)
            weigh(u - 2)
            for j in range(per):
                core_copy(t + j).start()

        i = t - chunks + loads - 2

        @pl.when((t >= chunks) & (i < 2 * loads))
        def _():
            inside_wait(i)
            apply(i - 1)
            weigh(i)

        @pl.when(i == 2 * loads)
        def _():
            apply(i - 1)

        @pl.when(states)
        def _():
            across_wait(a)
            across(a)

        return carry

    lax.fori_loop(3 * per, steps, step, 0)

    mean = jnp.sum(ssq_s[...], axis=1, keepdims=True) * (1.0 / (heads * D))
    ssq_s[...] = jnp.broadcast_to(lax.rsqrt(mean + EPS), (tok, D))

    for s in range(hn // g):
        h = me * hn + s * g
        src = (planes - 1) * GROUP + ((h // span) % 2) * 2 + (h % half) // w

        @pl.when(src != me)
        def _():
            send(
                s_out.at[0, pl.ds(0, g)], fin_s.at[pl.ds(s * g, g)], f_ss, f_rs.at[s], core_peer
            ).wait_recv()

    fac_core_copy().wait_send()
    fac_pair_copy().wait_send()
    send(u_own.at[:, 1 - c], u_core, core_ss, core_rs.at[0], core_peer).wait_send()
    send(u_send, u_pair, pair_ss, pair_rs.at[0], pair_peer).wait_send()

    @pl.when((plane > 0) | (y == 0))
    def _():
        send(e_send, s_in, e_ss, e_rs.at[0], pair_peer).wait_send()

    send(x_send, e_half, x_ss, x_rs.at[0], core_peer).wait_send()

    @pl.when(plane < planes - 1)
    def _():
        send(s_out, s_in, z_ss, z_rs.at[0], (me + GROUP) % n).wait_send()

    @pl.when(plane == planes - 1)
    def _():
        sent = pl.ds(0, chunks - max(1, hn // (2 * w)))
        send(s_out.at[sent], s_in.at[sent], f_ss, f_rs.at[0], core_peer).wait_send()


def finish_kernel(mix_ref, inv_ref, fin_in, out_hbm, fin_hbm, buf, fin_s, sem, fin_sem):
    parts = buf.shape[0]
    rows = buf.shape[1]
    fin_s[...] = fin_in[...].astype(F32)
    fin_copy = pltpu.make_async_copy(fin_s, fin_hbm, fin_sem)
    fin_copy.start()
    copies = [fin_copy]
    for p in range(parts):
        at = slice(p * rows, (p + 1) * rows)
        inv = inv_ref[at, :]
        for t in range(mix_ref.shape[1] // D):
            cols = slice(t * D, (t + 1) * D)
            buf[p, :, cols] = (mix_ref[at, cols].astype(F32) * inv).astype(BF16)
        copy = pltpu.make_async_copy(buf.at[p], out_hbm.at[pl.ds(p * rows, rows)], sem.at[p])
        copy.start()
        copies.append(copy)
    for copy in copies:
        copy.wait()


def shards(n, queries, keys_in, values_in, log_decay, gate_logits, norm_gain, doc_lengths):
    tok, width = queries.shape
    heads = width // D
    chunks = CHUNKS
    hc = heads // chunks
    half = hc // 2
    w = half // 2
    hn = heads // n
    g = math.gcd(w, hn)
    vm = pltpu.VMEM
    dma = pltpu.SemaphoreType.DMA
    anyspace = pl.BlockSpec(memory_space=pl.ANY)
    vspec = pl.BlockSpec(memory_space=pltpu.VMEM)
    part = vm((chunks, w, D, D), BF16)
    fac = vm((2, 2, chunks * w, D), F32)
    scratch = [
        vm((tok, width), F32), vm((tok, width), F32),
        vm((2, tok, width), BF16), vm((2, tok, width), BF16),
        vm((heads, D, tok), BF16), vm((max(heads, D), tok), BF16), vm((1, width), F32),
        pltpu.SMEM(doc_lengths.shape, jnp.int32),
        vm((tok, tok), F32), vm((heads, tok), F32), vm((heads, tok), F32), vm((tok, D), F32), vm((tok, D), F32),
        fac, fac, fac, vm((chunks * w, D), F32),
        vm((hc // 4 * (chunks // LOADS), 3, tok // 2, tok), BF16),
        vm((chunks, 2, 2, w, D, D), BF16), vm((chunks, 2, w, D, D), BF16), vm((chunks, w, D, D), F32),
        part, part, part, part, part,
        vm((chunks, 2, w, D, D), BF16), vm((chunks, 2, w, D, D), BF16),
        vm((chunks, 2, 2, w, D, D), BF16),
        dma((LOADS,)), dma((3,)), dma((2,)), dma((2,)),
        dma, dma((chunks,)), dma, dma((chunks,)), dma, dma((chunks,)), dma, dma((chunks,)), dma, dma((LOADS,)),
        dma, dma((hn // g,)), dma,
    ]
    mixed, squares, final = pl.pallas_call(
        functools.partial(kernel, n, heads, chunks),
        out_shape=(
            pltpu.VMEM((tok, width), BF16),
            pltpu.VMEM((tok, D), F32),
            pltpu.VMEM((hn, D, D), BF16),
        ),
        in_specs=[anyspace] * 7,
        out_specs=(vspec, vspec, vspec),
        scratch_shapes=scratch,
        compiler_params=pltpu.CompilerParams(
            collective_id=0, has_side_effects=True, vmem_limit_bytes=54 * 1024 * 1024
        ),
    )(queries, keys_in, values_in, gate_logits, log_decay.T, norm_gain.reshape(1, width), doc_lengths)
    rows = tok // FINISH_PARTS
    return pl.pallas_call(
        finish_kernel,
        out_shape=(
            jax.ShapeDtypeStruct((tok, width), BF16),
            jax.ShapeDtypeStruct((hn, D, D), F32),
        ),
        in_specs=[vspec, vspec, vspec],
        out_specs=(anyspace, anyspace),
        scratch_shapes=[
            vm((FINISH_PARTS, rows, width), BF16), vm((hn, D, D), F32), dma((FINISH_PARTS,)), dma,
        ],
        compiler_params=pltpu.CompilerParams(vmem_limit_bytes=16 * 1024 * 1024),
    )(mixed, squares, final)


def solution(mesh):
    rows = P(("grp", "seq"), None)
    return jax.shard_map(
        functools.partial(shards, mesh.shape["seq"]),
        mesh=mesh,
        in_specs=(rows, rows, rows, rows, rows, P(), P("grp")),
        out_specs=(rows, P(("grp", "seq"), None, None)),
        check_vma=False,
    )
```
